512 devices in a mesh: band: 8 (over y, core), space: 64 (over z, x).
Axes of the slice: x: 4, y: 4, z: 16, core: 2. Of those that a mesh axis runs over, the one named last changes fastest.
Arguments:
- snapshots: float32 [1152, 8, 32768], P(None, 'band', 'space'), may hold values from -6 to 6
- quad_weights: float32 [8, 32768], P('band', 'space'), may hold values from 0.2 to 9, as said below
- freq_bins: int32 [16], replicated, may hold values from 1 to 127, as said below
- block_starts: int32 [8], replicated, may hold values from 0 to 896, as said below
Outputs:
- factor: float32 [16, 2, 8, 8], P('band')
- modes: float32 [16, 2, 8, 8, 32768], P('band', None, None, None, 'space')
The draws below stay inside these ranges and needn't reach their ends.
Inputs may be any that keep to these rules, and one draw needn't show every extreme that they name: `freq_bins`: distinct and increasing; the first is 1 and the last is 127. `block_starts`: Increasing; the first is 0 and the last is 896; consecutive starts differ by 64 to 192. `quad_weights`: Positive.
All inputs are finite; a program needn't handle non-finite values.
Results may differ from the reference program's by a relative error of at most 0.000075.
Values sent between devices are 32-bit elements; how exact they have to be, the bound alone decides.
A program may use at most 64 MiB of HBM per device.

```python
import math
import jax
import jax.numpy as jnp
from jax import lax

BLOCK = 256
NBLK = 8
NFREQ = 16
SLABS = 8
TIMES = 1152
SLAB = 32768
NSPACE = 262144


def draw_freq_bins(key, part):
    inner = jax.random.permutation(key, BLOCK // 2 - 3)[:NFREQ - 2] + 2
    ends = jnp.array([1, BLOCK // 2 - 1], dtype=jnp.int32)
    return jnp.sort(jnp.concatenate([ends, inner.astype(jnp.int32)])).astype(jnp.int32)


def draw_block_starts(key, part):
    jitter = jax.random.randint(key, (NBLK - 2,), -(BLOCK // 8), BLOCK // 8 + 1)
    middle = jnp.arange(1, NBLK - 1).astype(jnp.int32) * (BLOCK // 2) + jitter.astype(jnp.int32)
    first = jnp.zeros((1,), jnp.int32)
    last = jnp.full((1,), (NBLK - 1) * (BLOCK // 2), jnp.int32)
    return jnp.concatenate([first, middle, last]).astype(jnp.int32)


def draw_quad_weights(key, part):
    ramp = jnp.arange(SLAB).astype(jnp.float32) / SLAB
    spread = jax.random.uniform(key, (SLABS, SLAB), jnp.float32, jnp.log(0.3), jnp.log(3.0))
    return jnp.exp(jnp.log(3.0) * ramp)[None, :] * jnp.exp(spread)


def level_of(key, shape, pieces, smallest, high):
    factor_of = 1.0
    for axis_at, parts in pieces:
        heights = jax.random.uniform(jax.random.fold_in(jax.random.fold_in(key, 6), axis_at), (parts,), jnp.float32, smallest / len(pieces), high / len(pieces))
        factor_of = factor_of * jnp.repeat(jnp.exp(heights), shape[axis_at] // parts).reshape((-1,) + (1,) * (len(shape) - 1 - axis_at))
    return factor_of


def bell_draw(rng, shape, deviation, limit, split=(), kind=jnp.bfloat16):
    entries = jax.random.normal(rng, shape, jnp.float32) * deviation
    if len(split) > 0:
        entries = level_of(rng, shape, split, -0.22, 0.18) * entries
    return jnp.clip(entries, min=-limit, max=limit).astype(kind)


def setup_inputs(seed: int = 0) -> dict:
    keys = jax.random.split(jax.random.key(seed), 5)
    snapshots = bell_draw(keys[0], (TIMES, SLABS, SLAB), 1.0, 6.0, ((1, 8), (2, 64)), jnp.float32)
    quad_weights = draw_quad_weights(jax.random.fold_in(keys[4], 71), 0)
    freq_bins = draw_freq_bins(jax.random.fold_in(keys[4], 71), 0)
    block_starts = draw_block_starts(jax.random.fold_in(keys[4], 71), 0)
    return {"snapshots": snapshots, "quad_weights": quad_weights, "freq_bins": freq_bins, "block_starts": block_starts}


def spectral_table(freq_bins, block_starts, total_times):
    moments = jnp.arange(total_times).astype(jnp.int32)
    offset = moments[None, :] - block_starts.astype(jnp.int32)[:, None]
    inside = (offset >= 0) & (offset < BLOCK)
    position = offset.astype(jnp.float32)
    taper = 0.5 - 0.5 * jnp.cos(2.0 * math.pi * position / BLOCK)
    turns = jnp.mod(freq_bins.astype(jnp.int32)[:, None, None] * offset[None, :, :], BLOCK).astype(jnp.float32)
    phase = 2.0 * math.pi * turns / BLOCK
    scaled = jnp.where(inside, taper, 0.0)[None] / math.sqrt(0.375 * BLOCK)
    table = jnp.stack([scaled * jnp.cos(phase), -scaled * jnp.sin(phase)], axis=1)
    return table.reshape(-1, total_times)

def spectra(snap_rows, weights, table):
    fluct = snap_rows - lax.optimization_barrier(jnp.mean(snap_rows, axis=0, keepdims=True))
    coeffs = jnp.dot(table, fluct, precision=lax.Precision.HIGHEST, preferred_element_type=jnp.float32)
    return coeffs * jnp.sqrt(weights)[None, :]

def gram_split(moment):
    half = moment.shape[-1] // 2
    real_part = moment[:, :half, :half] + moment[:, half:, half:]
    imag_part = moment[:, :half, half:] - moment[:, half:, :half]
    return (real_part, imag_part)

def factor_pair(gram_real, gram_imag):
    order = gram_real.shape[-1]
    columns = jnp.arange(order)
    rows_real = []
    rows_imag = []
    for pivot_row in range(order):
        left_real = gram_real[:, pivot_row, :]
        left_imag = gram_imag[:, pivot_row, :]
        for earlier in range(pivot_row):
            coef_real = rows_real[earlier][:, pivot_row:pivot_row + 1]
            coef_imag = rows_imag[earlier][:, pivot_row:pivot_row + 1]
            left_real = left_real - (coef_real * rows_real[earlier] + coef_imag * rows_imag[earlier])
            left_imag = left_imag - (coef_real * rows_imag[earlier] - coef_imag * rows_real[earlier])
        pivot = jnp.sqrt(left_real[:, pivot_row:pivot_row + 1])
        rows_real.append(jnp.where(columns >= pivot_row, left_real / pivot, 0.0))
        rows_imag.append(jnp.where(columns > pivot_row, left_imag / pivot, 0.0))
    return (jnp.stack(rows_real, 1), jnp.stack(rows_imag, 1))

def invert_pair(fac_real, fac_imag):
    order = fac_real.shape[-1]
    identity = jnp.eye(order, dtype=fac_real.dtype)
    inv_real = [None] * order
    inv_imag = [None] * order
    for target in reversed(range(order)):
        acc_real = jnp.broadcast_to(identity[target], fac_real[:, 0, :].shape)
        acc_imag = jnp.zeros_like(acc_real)
        for later in range(target + 1, order):
            coef_real = fac_real[:, target, later:later + 1]
            coef_imag = fac_imag[:, target, later:later + 1]
            acc_real = acc_real - (coef_real * inv_real[later] - coef_imag * inv_imag[later])
            acc_imag = acc_imag - (coef_real * inv_imag[later] + coef_imag * inv_real[later])
        diagonal = fac_real[:, target, target:target + 1]
        inv_real[target] = acc_real / diagonal
        inv_imag[target] = acc_imag / diagonal
    return (jnp.stack(inv_real, 1), jnp.stack(inv_imag, 1))

def make_kernel(inv_real, inv_imag):
    upper = jnp.stack([inv_real, inv_imag], 2)
    lower = jnp.stack([-inv_imag, inv_real], 2)
    return jnp.stack([upper, lower], 1)

def reference(snapshots, quad_weights, freq_bins, block_starts):
    table = spectral_table(freq_bins, block_starts, TIMES)

    def per_slab(index):
        snap_rows = lax.dynamic_index_in_dim(snapshots, index, 1, False)
        weights = lax.dynamic_index_in_dim(quad_weights, index, 0, False)
        return spectra(snap_rows, weights, table).reshape(NFREQ, 2, NBLK, SLAB)
    coeffs = lax.map(per_slab, jnp.arange(SLABS).astype(jnp.int32))
    vectors = coeffs.reshape(SLABS, NFREQ, 2 * NBLK, SLAB)
    moment = jnp.einsum('lfas,lfbs->fab', vectors, vectors, precision=lax.Precision.HIGHEST) / NSPACE
    fac_real, fac_imag = factor_pair(*gram_split(moment))
    inv_real, inv_imag = invert_pair(fac_real, fac_imag)
    kernel = make_kernel(inv_real, inv_imag)
    modes = jnp.einsum('fpacb,lfpas->fcbls', kernel, coeffs, precision=lax.Precision.HIGHEST)
    return (jnp.stack([fac_real, fac_imag], 1), modes)
```

```python
import functools
import math

import jax
import jax.numpy as jnp
from jax import lax
from jax.experimental import pallas as pl
from jax.experimental.pallas import tpu as pltpu
from jax.sharding import PartitionSpec as P

BLOCK = 256
NBLK = 8
NFREQ = 16
SLABS = 8
TIMES = 1152
CELLS = 512
LANES = 128
TILES = CELLS // LANES
ROWS = 2 * NFREQ * NBLK
HALF = NFREQ * NBLK
ALONG_X = 4
MESH = pl.DeviceIdType.MESH
CHUNKS = 4


def turn_parts(turns):
    quadrant = jnp.bitwise_and(jnp.right_shift(turns + 32, 6), 3)
    rest = jnp.bitwise_and(turns + 32, 63) - 32
    angle = rest.astype(jnp.float32) * (math.pi / 128.0)
    square = angle * angle
    sine = angle + angle * square * (
        -1.6666654611e-1 + square * (8.3321608736e-3 - 1.9515295891e-4 * square)
    )
    cosine = (1.0 - 0.5 * square) + square * square * (
        4.166664568298827e-2
        + square * (-1.388731625493765e-3 + 2.443315711809948e-5 * square)
    )
    odd = jnp.bitwise_and(quadrant, 1) == 1
    first = jnp.where(odd, sine, cosine)
    second = jnp.where(odd, cosine, sine)
    flip_cos = (quadrant == 1) | (quadrant == 2)
    flip_sin = quadrant >= 2
    return jnp.where(flip_cos, -first, first), jnp.where(flip_sin, -second, second)


def split(value):
    high = value.astype(jnp.bfloat16)
    low = (value - high.astype(jnp.float32)).astype(jnp.bfloat16)
    return high, low


def spectra_kernel(
    along_z,
    along_x,
    snap,
    weights,
    bins,
    starts,
    grouped,
    total,
    xbuf,
    table_high,
    table_low,
    x_high,
    x_low,
    coef_high,
    coef_low,
    outbox,
    row_out,
    row_in,
    far_out,
    far_in,
    load_sem,
    mine_sem,
    row_send,
    row_recv,
    far_send,
    far_recv,
    box_send,
    box_recv,
):
    band = lax.axis_index("band")
    space = lax.axis_index("space")
    z_at = space // along_x
    x_at = space % along_x
    bands = SLABS
    plane = along_x * bands
    me = x_at * bands + band

    def plane_peer(step):
        peer = lax.rem(me + step, plane)
        return peer % bands, (peer % bands, z_at * along_x + peer // bands)

    def far_peer(step):
        return (band, lax.rem(z_at + step, along_z) * along_x + x_at)

    piece = TIMES * TILES // CHUNKS
    loads = []
    for part in range(CHUNKS):
        load = pltpu.make_async_copy(
            snap.at[pl.ds(part * piece, piece)],
            xbuf.at[pl.ds(part * piece, piece)],
            load_sem.at[part],
        )
        load.start()
        loads.append(load)

    barrier = pltpu.get_barrier_semaphore()
    for step in range(1, along_z):
        pl.semaphore_signal(barrier, inc=1, device_id=far_peer(step), device_id_type=MESH)
    for step in range(1, plane):
        pl.semaphore_signal(
            barrier, inc=1, device_id=plane_peer(step)[1], device_id_type=MESH
        )

    shape = (2 * NBLK, TIMES)
    row = lax.broadcasted_iota(jnp.int32, shape, 0)
    moment = lax.broadcasted_iota(jnp.int32, shape, 1)
    offset = moment
    for block in range(NBLK):
        offset = jnp.where(
            jnp.bitwise_and(row, NBLK - 1) == block, moment - starts[block], offset
        )
    inside = (offset >= 0) & (offset < BLOCK)
    wave, _ = turn_parts(jnp.bitwise_and(offset, BLOCK - 1))
    scaled = jnp.where(inside, 0.5 - 0.5 * wave, 0.0) / math.sqrt(0.375 * BLOCK)

    def fill(pair, carry):
        bin_of = jnp.where(row < NBLK, bins[2 * pair], bins[2 * pair + 1])
        cosine, sine = turn_parts(jnp.bitwise_and(bin_of * offset, BLOCK - 1))
        at = pl.multiple_of(pair * 2 * NBLK, 2 * NBLK)
        for low_row, value in ((0, scaled * cosine), (HALF, -(scaled * sine))):
            high, low = split(value)
            table_high[pl.ds(low_row + at, 2 * NBLK), :] = high
            table_low[pl.ds(low_row + at, 2 * NBLK), :] = low
        return carry

    lax.fori_loop(0, NFREQ // 2, fill, 0)

    sums = jnp.zeros((32, LANES), jnp.float32)
    for part in range(CHUNKS):
        loads[part].wait()

        def gather(index, acc, part=part):
            at = pl.multiple_of(part * piece + index * 32, 32)
            return acc + xbuf[pl.ds(at, 32), :]

        sums = lax.fori_loop(0, piece // 32, gather, sums, unroll=4)
    sums = (sums[0:8] + sums[8:16]) + (sums[16:24] + sums[24:32])
    mean = (sums[0:4] + sums[4:8]) * (1.0 / TIMES)

    def reduce_mean(index, carry):
        at = pl.multiple_of(index * 32, 32)
        for tile in range(TILES):
            value = xbuf[pl.ds(at * TILES + tile, 32, stride=TILES), :]
            high, low = split(value - mean[tile : tile + 1, :])
            x_high[pl.ds(at, 32), tile * LANES : (tile + 1) * LANES] = high
            x_low[pl.ds(at, 32), tile * LANES : (tile + 1) * LANES] = low
        return carry

    lax.fori_loop(0, TIMES // 32, reduce_mean, 0, unroll=2)

    root = jnp.sqrt(weights[...])
    for side in range(2):
        lanes = slice(side * 256, side * 256 + 256)
        scale = jnp.concatenate(
            [root[2 * side : 2 * side + 1, :], root[2 * side + 1 : 2 * side + 2, :]], axis=1
        )
        coef = jnp.dot(table_high[...], x_high[:, lanes], preferred_element_type=jnp.float32)
        coef += jnp.dot(table_low[...], x_high[:, lanes], preferred_element_type=jnp.float32)
        coef += jnp.dot(table_high[...], x_low[:, lanes], preferred_element_type=jnp.float32)
        coef = coef * scale
        high, low = split(coef)
        coef_high[:, lanes] = high
        coef_low[:, lanes] = low
        for part in range(2):
            for freq in range(NFREQ):
                for tile in range(2):
                    value = coef[
                        part * HALF + freq * NBLK : part * HALF + (freq + 1) * NBLK,
                        tile * LANES : (tile + 1) * LANES,
                    ]
                    base = part * 64 + (freq % 2) * TILES + 2 * side + tile
                    outbox[freq // 2, pl.ds(base, NBLK, stride=8), :] = value

    across = (((1,), (1,)), ((), ()))
    gram = lax.dot_general(
        coef_high[...], coef_high[...], across, preferred_element_type=jnp.float32
    )
    gram += lax.dot_general(
        coef_low[...], coef_high[...], across, preferred_element_type=jnp.float32
    )
    gram += lax.dot_general(
        coef_high[...], coef_low[...], across, preferred_element_type=jnp.float32
    )
    tile_shape = (NBLK, LANES)
    sub = lax.broadcasted_iota(jnp.int32, tile_shape, 0)
    lane = lax.broadcasted_iota(jnp.int32, tile_shape, 1)
    real = jnp.zeros(tile_shape, jnp.float32)
    imag = jnp.zeros(tile_shape, jnp.float32)
    for freq in range(NFREQ):
        up = slice(freq * NBLK, (freq + 1) * NBLK)
        down = slice(HALF + freq * NBLK, HALF + (freq + 1) * NBLK)
        own = jnp.right_shift(lane, 3) == freq
        real = jnp.where(own, gram[up, :HALF] + gram[down, HALF:], real)
        imag = jnp.where(own, gram[up, HALF:] - gram[down, :HALF], imag)
    count = SLABS * CELLS * along_x * along_z
    packed = jnp.where(sub <= jnp.bitwise_and(lane, 7), real, imag) * (1.0 / count)
    diagonal = jnp.right_shift(lane, 4) == sub
    rows = jnp.where(diagonal, packed, 0.0)
    for step in range(1, 8):
        turned = jnp.where(diagonal, pltpu.roll(packed, 16 * step, 1), 0.0)
        rows = rows + pltpu.roll(turned, 8 - step, 0)
    row_out[...] = rows.reshape(NBLK, 1, LANES)
    row_in[me] = row_out[band]

    pl.semaphore_wait(barrier, plane - 1 + along_z - 1)

    row_copies = []
    for step in range(1, plane):
        peer_band, peer = plane_peer(step)
        copy = pltpu.make_async_remote_copy(
            src_ref=row_out.at[peer_band],
            dst_ref=row_in.at[me],
            send_sem=row_send,
            recv_sem=row_recv,
            device_id=peer,
            device_id_type=MESH,
        )
        copy.start()
        row_copies.append(copy)
    mine = pltpu.make_async_copy(outbox.at[band], grouped.at[band], mine_sem)
    mine.start()
    box_copies = []
    for step in (4, 3, 5, 2, 6, 1, 7):
        peer_band = lax.rem(band + step, bands)
        copy = pltpu.make_async_remote_copy(
            src_ref=outbox.at[peer_band],
            dst_ref=grouped.at[band],
            send_sem=box_send,
            recv_sem=box_recv,
            device_id=(peer_band, space),
            device_id_type=MESH,
        )
        copy.start()
        box_copies.append(copy)

    arrived = row_in.at[pl.ds(0, plane - 1)]
    pltpu.make_async_copy(arrived, arrived, row_recv).wait()
    near = jnp.sum(row_in[...], axis=0)
    far_out[...] = near.reshape(1, 1, LANES)
    far_in[z_at] = near

    far_copies = []
    for step in sorted(range(1, along_z), key=lambda s: -min(s, along_z - s)):
        copy = pltpu.make_async_remote_copy(
            src_ref=far_out.at[0],
            dst_ref=far_in.at[z_at],
            send_sem=far_send,
            recv_sem=far_recv,
            device_id=far_peer(step),
            device_id_type=MESH,
        )
        copy.start()
        far_copies.append(copy)
    pltpu.make_async_copy(arrived, arrived, row_send).wait()
    arrived = far_in.at[pl.ds(0, along_z - 1)]
    pltpu.make_async_copy(arrived, arrived, far_recv).wait()
    total[...] = jnp.broadcast_to(jnp.sum(far_in[...], axis=0), (8, LANES))
    pltpu.make_async_copy(arrived, arrived, far_send).wait()
    mine.wait()
    arrived = grouped.at[pl.ds(0, bands - 1)]
    pltpu.make_async_copy(arrived, arrived, box_recv).wait()
    arrived = outbox.at[pl.ds(0, bands - 1)]
    pltpu.make_async_copy(arrived, arrived, box_send).wait()


def modes_kernel(total, grouped, factor, modes, held, out_sem):
    shape = (NBLK, LANES)
    sub = lax.broadcasted_iota(jnp.int32, shape, 0)
    lane = lax.broadcasted_iota(jnp.int32, shape, 1)
    packed = total[...]
    packed = jnp.where(sub < 4, packed, pltpu.roll(packed, LANES - 8, 1))

    def entry(r, c):
        return jnp.broadcast_to(packed[:, 16 * r + c : 16 * r + c + 1], shape)

    order = NBLK
    gram_real = {(r, c): entry(r, c) for r in range(order) for c in range(r, order)}
    gram_imag = {(r, c): -entry(c, r) for r in range(order) for c in range(r + 1, order)}
    inv_real, inv_imag = {}, {}
    fac = [jnp.zeros(shape, jnp.float32), jnp.zeros(shape, jnp.float32)]
    copies = []
    for k in range(order):
        pivot = gram_real[k, k]
        scale = lax.rsqrt(pivot)
        scale = scale * (1.5 - 0.5 * pivot * scale * scale)
        row_real, row_imag = {}, {}
        for c in range(k + 1, order):
            row_real[c] = gram_real[k, c] * scale
            row_imag[c] = gram_imag[k, c] * scale
        fac[0] = jnp.where(lane == 8 * k + k, pivot * scale, fac[0])
        for c in range(k + 1, order):
            fac[0] = jnp.where(lane == 8 * k + c, row_real[c], fac[0])
            fac[1] = jnp.where(lane == 8 * k + c, row_imag[c], fac[1])
        for i in range(k + 1, order):
            gram_real[i, i] = gram_real[i, i] - (
                row_real[i] * row_real[i] + row_imag[i] * row_imag[i]
            )
            for c in range(i + 1, order):
                gram_real[i, c] = gram_real[i, c] - (
                    row_real[i] * row_real[c] + row_imag[i] * row_imag[c]
                )
                gram_imag[i, c] = gram_imag[i, c] - (
                    row_real[i] * row_imag[c] - row_imag[i] * row_real[c]
                )
        for m in range(k):
            inv_real[k, m] = inv_real[k, m] * scale
            inv_imag[k, m] = inv_imag[k, m] * scale
        inv_real[k, k] = scale
        for i in range(k + 1, order):
            for m in range(k):
                inv_real[i, m] = inv_real[i, m] - (
                    row_real[i] * inv_real[k, m] + row_imag[i] * inv_imag[k, m]
                )
                inv_imag[i, m] = inv_imag[i, m] - (
                    row_real[i] * inv_imag[k, m] - row_imag[i] * inv_real[k, m]
                )
            inv_real[i, k] = -(row_real[i] * scale)
            inv_imag[i, k] = row_imag[i] * scale
        for slab in range(SLABS):
            real = inv_real[k, k] * grouped[slab, pl.ds(k * 8, 8), :]
            imag = inv_real[k, k] * grouped[slab, pl.ds(64 + k * 8, 8), :]
            for a in range(k):
                part_real = grouped[slab, pl.ds(a * 8, 8), :]
                part_imag = grouped[slab, pl.ds(64 + a * 8, 8), :]
                real = real + (inv_real[k, a] * part_real + inv_imag[k, a] * part_imag)
                imag = imag + (inv_real[k, a] * part_imag - inv_imag[k, a] * part_real)
            held[k, pl.ds(slab, 8, stride=8), :] = real
            held[8 + k, pl.ds(slab, 8, stride=8), :] = imag
        for p in range(2):
            for f in range(2):
                copy = pltpu.make_async_copy(
                    held.at[p * 8 + k, pl.ds(f * 32, 32)],
                    modes.at[f, p * 8 + k],
                    out_sem.at[k * 4 + p * 2 + f],
                )
                copy.start()
                copies.append(copy)
    for p in range(2):
        for f in range(2):
            line = jnp.broadcast_to(fac[p][4 * f : 4 * f + 1, :], shape)
            tile = line
            for r in range(1, order):
                tile = jnp.where(sub == r, pltpu.roll(line, LANES - 8 * r, 1), tile)
            factor[f, p] = tile[:, :8]
    for copy in copies:
        copy.wait()


def shards(along_z, along_x, snapshots, quad_weights, freq_bins, block_starts):
    f32, bf16 = jnp.float32, jnp.bfloat16
    vmem = pltpu.VMEM
    dma = pltpu.SemaphoreType.DMA
    bands = SLABS
    grouped, total = pl.pallas_call(
        functools.partial(spectra_kernel, along_z, along_x),
        out_shape=(
            jax.ShapeDtypeStruct((bands, 128, LANES), f32),
            jax.ShapeDtypeStruct((8, LANES), f32),
        ),
        in_specs=[
            pl.BlockSpec(memory_space=pl.ANY),
            pl.BlockSpec(memory_space=pltpu.VMEM),
            pl.BlockSpec(memory_space=pltpu.SMEM),
            pl.BlockSpec(memory_space=pltpu.SMEM),
        ],
        out_specs=(
            pl.BlockSpec(memory_space=pl.ANY),
            pl.BlockSpec(memory_space=pltpu.VMEM),
        ),
        scratch_shapes=[
            vmem((TIMES * TILES, LANES), f32),
            vmem((ROWS, TIMES), bf16),
            vmem((ROWS, TIMES), bf16),
            vmem((TIMES, CELLS), bf16),
            vmem((TIMES, CELLS), bf16),
            vmem((ROWS, CELLS), bf16),
            vmem((ROWS, CELLS), bf16),
            vmem((bands, 128, LANES), f32),
            vmem((bands, 1, LANES), f32),
            vmem((along_x * bands, 1, LANES), f32),
            vmem((1, 1, LANES), f32),
            vmem((along_z, 1, LANES), f32),
            dma((CHUNKS,)),
            dma,
            dma,
            dma,
            dma,
            dma,
            dma,
            dma,
        ],
        compiler_params=pltpu.CompilerParams(collective_id=0, has_side_effects=True),
        name="spectra",
    )(
        snapshots.reshape(TIMES * TILES, LANES),
        quad_weights.reshape(TILES, LANES),
        freq_bins,
        block_starts,
    )
    factor, modes = pl.pallas_call(
        modes_kernel,
        out_shape=(
            jax.ShapeDtypeStruct((2, 2, NBLK, NBLK), f32),
            jax.ShapeDtypeStruct((2, 16, 32, LANES), f32),
        ),
        in_specs=[
            pl.BlockSpec(memory_space=pltpu.VMEM),
            pl.BlockSpec(memory_space=pltpu.VMEM),
        ],
        out_specs=(
            pl.BlockSpec(memory_space=pltpu.VMEM),
            pl.BlockSpec(memory_space=pl.ANY),
        ),
        scratch_shapes=[vmem((16, 64, LANES), f32), dma((32,))],
        name="modes",
    )(total, grouped)
    modes = modes.reshape(2, 2, NBLK, TILES, SLABS, LANES).transpose(0, 1, 2, 4, 3, 5)
    return (factor, modes.reshape(2, 2, NBLK, SLABS, CELLS))


def solution(mesh):
    along_x = min(ALONG_X, mesh.shape["space"])
    along_z = mesh.shape["space"] // along_x
    placed = (P(None, "band", "space"), P("band", "space"), P(), P())
    return jax.shard_map(
        functools.partial(shards, along_z, along_x),
        mesh=mesh,
        in_specs=placed,
        out_specs=(P("band", None, None, None), P("band", None, None, None, "space")),
        check_vma=False,
    )
```

```python
import functools
import math

import jax
import jax.numpy as jnp
from jax import lax
from jax.experimental import pallas as pl
from jax.experimental.pallas import tpu as pltpu
from jax.sharding import PartitionSpec as P

BLOCK = 256
NBLK = 8
NFREQ = 16
SLABS = 8
TIMES = 1152
CELLS = 512
LANES = 128
TILES = CELLS // LANES
ROWS = 2 * NFREQ * NBLK
HALF = NFREQ * NBLK
ALONG_X = 4
MESH = pl.DeviceIdType.MESH
CHUNKS = 4


def turn_parts(turns):
    quadrant = jnp.bitwise_and(jnp.right_shift(turns + 32, 6), 3)
    rest = jnp.bitwise_and(turns + 32, 63) - 32
    angle = rest.astype(jnp.float32) * (math.pi / 128.0)
    square = angle * angle
    sine = angle + angle * square * (
        -1.6666654611e-1 + square * (8.3321608736e-3 - 1.9515295891e-4 * square)
    )
    cosine = (1.0 - 0.5 * square) + square * square * (
        4.166664568298827e-2
        + square * (-1.388731625493765e-3 + 2.443315711809948e-5 * square)
    )
    odd = jnp.bitwise_and(quadrant, 1) == 1
    first = jnp.where(odd, sine, cosine)
    second = jnp.where(odd, cosine, sine)
    flip_cos = (quadrant == 1) | (quadrant == 2)
    flip_sin = quadrant >= 2
    return jnp.where(flip_cos, -first, first), jnp.where(flip_sin, -second, second)


def split(value):
    high = value.astype(jnp.bfloat16)
    low = (value - high.astype(jnp.float32)).astype(jnp.bfloat16)
    return high, low


def spectra_kernel(
    along_z,
    along_x,
    snap,
    weights_any,
    bins_any,
    starts_any,
    grouped,
    total,
    weights,
    bins,
    starts,
    xbuf,
    table_high,
    table_low,
    x_high,
    x_low,
    coef_high,
    coef_low,
    outbox,
    row_out,
    row_in,
    far_out,
    far_in,
    load_sem,
    small_sem,
    mine_sem,
    row_send,
    row_recv,
    far_send,
    far_recv,
    box_send,
    box_recv,
):
    band = lax.axis_index("band")
    space = lax.axis_index("space")
    z_at = space // along_x
    x_at = space % along_x
    bands = SLABS
    plane = along_x * bands
    me = x_at * bands + band

    def plane_peer(dx, dy, dc):
        x_to = lax.rem(x_at + dx, along_x)
        band_to = lax.rem(band // 2 + dy, bands // 2) * 2 + lax.rem(band % 2 + dc, 2)
        return band_to, (band_to, z_at * along_x + x_to)

    def far_peer(step):
        return (band, lax.rem(z_at + step, along_z) * along_x + x_at)

    def hops(step, size):
        return min(step, size - step)

    plane_steps = [
        (dx, dy, dc)
        for dx in range(along_x)
        for dy in range(bands // 2)
        for dc in range(2)
        if dx + dy + dc > 0
    ]
    plane_steps.sort(key=lambda s: -hops(s[0], along_x) - hops(s[1], bands // 2))
    far_steps = sorted(range(1, along_z), key=lambda s: -hops(s, along_z))

    smalls = []
    for index, (source, target) in enumerate(
        ((starts_any, starts), (bins_any, bins), (weights_any, weights))
    ):
        load = pltpu.make_async_copy(source, target, small_sem.at[index])
        load.start()
        smalls.append(load)
    piece = TIMES * TILES // CHUNKS
    loads = []
    for part in range(CHUNKS):
        load = pltpu.make_async_copy(
            snap.at[pl.ds(part * piece, piece)],
            xbuf.at[pl.ds(part * piece, piece)],
            load_sem.at[part],
        )
        load.start()
        loads.append(load)

    barrier = pltpu.get_barrier_semaphore()
    for step in far_steps:
        pl.semaphore_signal(barrier, inc=1, device_id=far_peer(step), device_id_type=MESH)
    for step in plane_steps:
        pl.semaphore_signal(
            barrier, inc=1, device_id=plane_peer(*step)[1], device_id_type=MESH
        )
    for load in smalls:
        load.wait()

    shape = (2 * NBLK, TIMES)
    row = lax.broadcasted_iota(jnp.int32, shape, 0)
    moment = lax.broadcasted_iota(jnp.int32, shape, 1)
    offset = moment
    for block in range(NBLK):
        offset = jnp.where(
            jnp.bitwise_and(row, NBLK - 1) == block, moment - starts[block], offset
        )
    inside = (offset >= 0) & (offset < BLOCK)
    wave, _ = turn_parts(jnp.bitwise_and(offset, BLOCK - 1))
    scaled = jnp.where(inside, 0.5 - 0.5 * wave, 0.0) / math.sqrt(0.375 * BLOCK)

    def fill(pair, carry):
        bin_of = jnp.where(row < NBLK, bins[2 * pair], bins[2 * pair + 1])
        cosine, sine = turn_parts(jnp.bitwise_and(bin_of * offset, BLOCK - 1))
        at = pl.multiple_of(pair * 2 * NBLK, 2 * NBLK)
        for low_row, value in ((0, scaled * cosine), (HALF, -(scaled * sine))):
            high, low = split(value)
            table_high[pl.ds(low_row + at, 2 * NBLK), :] = high
            table_low[pl.ds(low_row + at, 2 * NBLK), :] = low
        return carry

    lax.fori_loop(0, NFREQ // 2, fill, 0)

    sums = jnp.zeros((32, LANES), jnp.float32)
    for part in range(CHUNKS):
        loads[part].wait()

        def gather(index, acc, part=part):
            at = pl.multiple_of(part * piece + index * 32, 32)
            return acc + xbuf[pl.ds(at, 32), :]

        sums = lax.fori_loop(0, piece // 32, gather, sums, unroll=4)
    sums = (sums[0:8] + sums[8:16]) + (sums[16:24] + sums[24:32])
    mean = (sums[0:4] + sums[4:8]) * (1.0 / TIMES)

    def reduce_mean(index, carry):
        at = pl.multiple_of(index * 32, 32)
        for tile in range(TILES):
            value = xbuf[pl.ds(at * TILES + tile, 32, stride=TILES), :]
            high, low = split(value - mean[tile : tile + 1, :])
            x_high[pl.ds(at, 32), tile * LANES : (tile + 1) * LANES] = high
            x_low[pl.ds(at, 32), tile * LANES : (tile + 1) * LANES] = low
        return carry

    lax.fori_loop(0, TIMES // 32, reduce_mean, 0, unroll=2)

    root = jnp.sqrt(weights[...])
    for side in range(2):
        lanes = slice(side * 256, side * 256 + 256)
        scale = jnp.concatenate(
            [root[2 * side : 2 * side + 1, :], root[2 * side + 1 : 2 * side + 2, :]], axis=1
        )
        coef = jnp.dot(table_high[...], x_high[:, lanes], preferred_element_type=jnp.float32)
        coef += jnp.dot(table_low[...], x_high[:, lanes], preferred_element_type=jnp.float32)
        coef += jnp.dot(table_high[...], x_low[:, lanes], preferred_element_type=jnp.float32)
        coef = coef * scale
        high, low = split(coef)
        coef_high[:, lanes] = high
        coef_low[:, lanes] = low
        for part in range(2):
            for freq in range(NFREQ):
                for tile in range(2):
                    value = coef[
                        part * HALF + freq * NBLK : part * HALF + (freq + 1) * NBLK,
                        tile * LANES : (tile + 1) * LANES,
                    ]
                    base = part * 64 + (freq % 2) * TILES + 2 * side + tile
                    outbox[freq // 2, pl.ds(base, NBLK, stride=8), :] = value

    across = (((1,), (1,)), ((), ()))
    gram = lax.dot_general(
        coef_high[...], coef_high[...], across, preferred_element_type=jnp.float32
    )
    gram += lax.dot_general(
        coef_low[...], coef_high[...], across, preferred_element_type=jnp.float32
    )
    gram += lax.dot_general(
        coef_high[...], coef_low[...], across, preferred_element_type=jnp.float32
    )
    tile_shape = (NBLK, LANES)
    sub = lax.broadcasted_iota(jnp.int32, tile_shape, 0)
    lane = lax.broadcasted_iota(jnp.int32, tile_shape, 1)
    real = jnp.zeros(tile_shape, jnp.float32)
    imag = jnp.zeros(tile_shape, jnp.float32)
    for freq in range(NFREQ):
        up = slice(freq * NBLK, (freq + 1) * NBLK)
        down = slice(HALF + freq * NBLK, HALF + (freq + 1) * NBLK)
        own = jnp.right_shift(lane, 3) == freq
        real = jnp.where(own, gram[up, :HALF] + gram[down, HALF:], real)
        imag = jnp.where(own, gram[up, HALF:] - gram[down, :HALF], imag)
    count = SLABS * CELLS * along_x * along_z
    packed = jnp.where(sub <= jnp.bitwise_and(lane, 7), real, imag) * (1.0 / count)
    diagonal = jnp.right_shift(lane, 4) == sub
    rows = jnp.where(diagonal, packed, 0.0)
    for step in range(1, 8):
        turned = jnp.where(diagonal, pltpu.roll(packed, 16 * step, 1), 0.0)
        rows = rows + pltpu.roll(turned, 8 - step, 0)
    row_out[...] = rows.reshape(NBLK, 1, LANES)
    row_in[me] = row_out[band]

    pl.semaphore_wait(barrier, plane - 1 + along_z - 1)

    row_copies = []
    for step in plane_steps:
        peer_band, peer = plane_peer(*step)
        copy = pltpu.make_async_remote_copy(
            src_ref=row_out.at[peer_band],
            dst_ref=row_in.at[me],
            send_sem=row_send,
            recv_sem=row_recv,
            device_id=peer,
            device_id_type=MESH,
        )
        copy.start()
        row_copies.append(copy)
    mine = pltpu.make_async_copy(outbox.at[band], grouped.at[band], mine_sem)
    mine.start()
    box_copies = []
    for step in (4, 3, 5, 2, 6, 1, 7):
        peer_band = lax.rem(band + step, bands)
        copy = pltpu.make_async_remote_copy(
            src_ref=outbox.at[peer_band],
            dst_ref=grouped.at[band],
            send_sem=box_send,
            recv_sem=box_recv,
            device_id=(peer_band, space),
            device_id_type=MESH,
        )
        copy.start()
        box_copies.append(copy)

    arrived = row_in.at[pl.ds(0, plane - 1)]
    pltpu.make_async_copy(arrived, arrived, row_recv).wait()
    near = jnp.sum(row_in[...], axis=0)
    far_out[...] = near.reshape(1, 1, LANES)
    far_in[z_at] = near

    far_copies = []
    for step in far_steps:
        copy = pltpu.make_async_remote_copy(
            src_ref=far_out.at[0],
            dst_ref=far_in.at[z_at],
            send_sem=far_send,
            recv_sem=far_recv,
            device_id=far_peer(step),
            device_id_type=MESH,
        )
        copy.start()
        far_copies.append(copy)
    pltpu.make_async_copy(arrived, arrived, row_send).wait()
    arrived = far_in.at[pl.ds(0, along_z - 1)]
    pltpu.make_async_copy(arrived, arrived, far_recv).wait()
    total[...] = jnp.broadcast_to(jnp.sum(far_in[...], axis=0), (8, LANES))
    pltpu.make_async_copy(arrived, arrived, far_send).wait()
    mine.wait()
    arrived = grouped.at[pl.ds(0, bands - 1)]
    pltpu.make_async_copy(arrived, arrived, box_recv).wait()
    arrived = outbox.at[pl.ds(0, bands - 1)]
    pltpu.make_async_copy(arrived, arrived, box_send).wait()


def modes_kernel(total, grouped, factor, modes, tiles, held, tile_sem, out_sem):
    shape = (NBLK, LANES)
    sub = lax.broadcasted_iota(jnp.int32, shape, 0)
    lane = lax.broadcasted_iota(jnp.int32, shape, 1)
    packed = total[...]
    packed = jnp.where(sub < 4, packed, pltpu.roll(packed, LANES - 8, 1))

    def entry(r, c):
        return jnp.broadcast_to(packed[:, 16 * r + c : 16 * r + c + 1], shape)

    order = NBLK
    gram_real = {(r, c): entry(r, c) for r in range(order) for c in range(r, order)}
    gram_imag = {(r, c): -entry(c, r) for r in range(order) for c in range(r + 1, order)}
    inv_real, inv_imag = {}, {}
    fac = [jnp.zeros(shape, jnp.float32), jnp.zeros(shape, jnp.float32)]
    copies = []
    for k in range(order):
        pivot = gram_real[k, k]
        scale = lax.rsqrt(pivot)
        scale = scale * (1.5 - 0.5 * pivot * scale * scale)
        row_real, row_imag = {}, {}
        for c in range(k + 1, order):
            row_real[c] = gram_real[k, c] * scale
            row_imag[c] = gram_imag[k, c] * scale
        fac[0] = jnp.where(lane == 8 * k + k, pivot * scale, fac[0])
        for c in range(k + 1, order):
            fac[0] = jnp.where(lane == 8 * k + c, row_real[c], fac[0])
            fac[1] = jnp.where(lane == 8 * k + c, row_imag[c], fac[1])
        for i in range(k + 1, order):
            gram_real[i, i] = gram_real[i, i] - (
                row_real[i] * row_real[i] + row_imag[i] * row_imag[i]
            )
            for c in range(i + 1, order):
                gram_real[i, c] = gram_real[i, c] - (
                    row_real[i] * row_real[c] + row_imag[i] * row_imag[c]
                )
                gram_imag[i, c] = gram_imag[i, c] - (
                    row_real[i] * row_imag[c] - row_imag[i] * row_real[c]
                )
        for m in range(k):
            inv_real[k, m] = inv_real[k, m] * scale
            inv_imag[k, m] = inv_imag[k, m] * scale
        inv_real[k, k] = scale
        for i in range(k + 1, order):
            for m in range(k):
                inv_real[i, m] = inv_real[i, m] - (
                    row_real[i] * inv_real[k, m] + row_imag[i] * inv_imag[k, m]
                )
                inv_imag[i, m] = inv_imag[i, m] - (
                    row_real[i] * inv_imag[k, m] - row_imag[i] * inv_real[k, m]
                )
            inv_real[i, k] = -(row_real[i] * scale)
            inv_imag[i, k] = row_imag[i] * scale
        for slab in range(SLABS):
            real = inv_real[k, k] * grouped[slab, pl.ds(k * 8, 8), :]
            imag = inv_real[k, k] * grouped[slab, pl.ds(64 + k * 8, 8), :]
            for a in range(k):
                part_real = grouped[slab, pl.ds(a * 8, 8), :]
                part_imag = grouped[slab, pl.ds(64 + a * 8, 8), :]
                real = real + (inv_real[k, a] * part_real + inv_imag[k, a] * part_imag)
                imag = imag + (inv_real[k, a] * part_imag - inv_imag[k, a] * part_real)
            held[k, 0, pl.ds(slab, 8, stride=8), :] = real
            held[k, 1, pl.ds(slab, 8, stride=8), :] = imag
        if k == order - 1:
            for p in range(2):
                for f in range(2):
                    line = jnp.broadcast_to(fac[p][4 * f : 4 * f + 1, :], shape)
                    tile = line
                    for r in range(1, order):
                        tile = jnp.where(sub == r, pltpu.roll(line, LANES - 8 * r, 1), tile)
                    tiles[f, p] = tile[:, :8]
            out = pltpu.make_async_copy(tiles, factor, tile_sem)
            out.start()
        for f in range(2):
            copy = pltpu.make_async_copy(
                held.at[k, :, pl.ds(f * 32, 32)],
                modes.at[f, :, k],
                out_sem,
            )
            copy.start()
    out.wait()
    pltpu.make_async_copy(modes, modes, out_sem).wait()


def shards(along_z, along_x, snapshots, quad_weights, freq_bins, block_starts):
    f32, bf16 = jnp.float32, jnp.bfloat16
    vmem = pltpu.VMEM
    dma = pltpu.SemaphoreType.DMA
    bands = SLABS
    grouped, total = pl.pallas_call(
        functools.partial(spectra_kernel, along_z, along_x),
        out_shape=(
            vmem((bands, 128, LANES), f32),
            vmem((8, LANES), f32),
        ),
        in_specs=[pl.BlockSpec(memory_space=pl.ANY)] * 4,
        out_specs=(pl.BlockSpec(memory_space=pltpu.VMEM), pl.BlockSpec(memory_space=pltpu.VMEM)),
        scratch_shapes=[
            vmem((TILES, LANES), f32),
            pltpu.SMEM((NFREQ,), jnp.int32),
            pltpu.SMEM((NBLK,), jnp.int32),
            vmem((TIMES * TILES, LANES), f32),
            vmem((ROWS, TIMES), bf16),
            vmem((ROWS, TIMES), bf16),
            vmem((TIMES, CELLS), bf16),
            vmem((TIMES, CELLS), bf16),
            vmem((ROWS, CELLS), bf16),
            vmem((ROWS, CELLS), bf16),
            vmem((bands, 128, LANES), f32),
            vmem((bands, 1, LANES), f32),
            vmem((along_x * bands, 1, LANES), f32),
            vmem((1, 1, LANES), f32),
            vmem((along_z, 1, LANES), f32),
            dma((CHUNKS,)),
            dma((3,)),
            dma,
            dma,
            dma,
            dma,
            dma,
            dma,
            dma,
        ],
        compiler_params=pltpu.CompilerParams(collective_id=0, has_side_effects=True),
        name="spectra",
    )(
        snapshots.reshape(TIMES * TILES, LANES),
        quad_weights.reshape(TILES, LANES),
        freq_bins,
        block_starts,
    )
    factor, modes = pl.pallas_call(
        modes_kernel,
        out_shape=(
            jax.ShapeDtypeStruct((2, 2, NBLK, NBLK), f32),
            jax.ShapeDtypeStruct((2, 2, NBLK, 32, LANES), f32),
        ),
        in_specs=[
            pl.BlockSpec(memory_space=pltpu.VMEM),
            pl.BlockSpec(memory_space=pltpu.VMEM),
        ],
        out_specs=(
            pl.BlockSpec(memory_space=pl.ANY),
            pl.BlockSpec(memory_space=pl.ANY),
        ),
        scratch_shapes=[
            vmem((2, 2, NBLK, NBLK), f32),
            vmem((NBLK, 2, 64, LANES), f32),
            dma,
            dma,
        ],
        name="modes",
    )(
        pltpu.with_memory_space_constraint(total, pltpu.VMEM),
        pltpu.with_memory_space_constraint(grouped, pltpu.VMEM),
    )
    modes = modes.reshape(2, 2, NBLK, TILES, SLABS, LANES).transpose(0, 1, 2, 4, 3, 5)
    return (factor, modes.reshape(2, 2, NBLK, SLABS, CELLS))


def solution(mesh):
    along_x = min(ALONG_X, mesh.shape["space"])
    along_z = mesh.shape["space"] // along_x
    placed = (P(None, "band", "space"), P("band", "space"), P(), P())
    return jax.shard_map(
        functools.partial(shards, along_z, along_x),
        mesh=mesh,
        in_specs=placed,
        out_specs=(P("band", None, None, None), P("band", None, None, None, "space")),
        check_vma=False,
    )
```

```python
import functools
import math

import jax
import jax.numpy as jnp
from jax import lax
from jax.experimental import pallas as pl
from jax.experimental.pallas import tpu as pltpu
from jax.sharding import PartitionSpec as P

BLOCK = 256
NBLK = 8
NFREQ = 16
SLABS = 8
TIMES = 1152
CELLS = 512
LANES = 128
TILES = CELLS // LANES
ROWS = 2 * NFREQ * NBLK
HALF = NFREQ * NBLK
ALONG_X = 4
MESH = pl.DeviceIdType.MESH
DEPTH = 256
STEPS = tuple((at, min(DEPTH, TIMES - at)) for at in range(0, TIMES, DEPTH))
LAST = TIMES - BLOCK
LEAST, MOST = 64, 192


def reach(block):
    first = max(LEAST * block, LAST - MOST * (NBLK - 1 - block))
    final = min(MOST * block, LAST - LEAST * (NBLK - 1 - block))
    return first, final + BLOCK


def active(at, size):
    return [b for b in range(NBLK) if reach(b)[0] < at + size and reach(b)[1] > at]


def turn_parts(turns):
    quadrant = jnp.bitwise_and(jnp.right_shift(turns + 32, 6), 3)
    rest = jnp.bitwise_and(turns + 32, 63) - 32
    angle = rest.astype(jnp.float32) * (math.pi / 128.0)
    square = angle * angle
    sine = angle + angle * square * (
        -1.6666654611e-1 + square * (8.3321608736e-3 - 1.9515295891e-4 * square)
    )
    cosine = (1.0 - 0.5 * square) + square * square * (
        4.166664568298827e-2
        + square * (-1.388731625493765e-3 + 2.443315711809948e-5 * square)
    )
    odd = jnp.bitwise_and(quadrant, 1) == 1
    first = jnp.where(odd, sine, cosine)
    second = jnp.where(odd, cosine, sine)
    flip_cos = (quadrant == 1) | (quadrant == 2)
    flip_sin = quadrant >= 2
    return jnp.where(flip_cos, -first, first), jnp.where(flip_sin, -second, second)


def split(value):
    high = value.astype(jnp.bfloat16)
    low = (value - high.astype(jnp.float32)).astype(jnp.bfloat16)
    return high, low


def spectra_kernel(
    along_z,
    along_x,
    snap,
    weights_any,
    bins_any,
    starts_any,
    grouped,
    total,
    weights,
    bins,
    starts,
    xbuf,
    tables,
    x_high,
    x_low,
    coef_sum,
    coef_high,
    coef_low,
    outbox,
    row_out,
    row_in,
    far_out,
    far_in,
    load_sem,
    small_sem,
    mine_sem,
    row_send,
    row_recv,
    far_send,
    far_recv,
    box_send,
    box_recv,
    met_sem,
):
    band = lax.axis_index("band")
    space = lax.axis_index("space")
    z_at = space // along_x
    x_at = space % along_x
    bands = SLABS
    plane = along_x * bands
    me = x_at * bands + band

    def plane_peer(dx, dy, dc):
        x_to = lax.rem(x_at + dx, along_x)
        band_to = lax.rem(band // 2 + dy, bands // 2) * 2 + lax.rem(band % 2 + dc, 2)
        return band_to, (band_to, z_at * along_x + x_to)

    def far_peer(step):
        return (band, lax.rem(z_at + step, along_z) * along_x + x_at)

    def hops(step, size):
        return min(step, size - step)

    plane_steps = [
        (dx, dy, dc)
        for dx in range(along_x)
        for dy in range(bands // 2)
        for dc in range(2)
        if dx + dy + dc > 0
    ]
    plane_steps.sort(key=lambda s: -hops(s[0], along_x) - hops(s[1], bands // 2))
    relay = max(1, along_z // 4)
    far_steps = sorted(range(1, along_z), key=lambda s: -hops(s, along_z))

    near_steps = [step for step in far_steps if hops(step, along_z) <= relay]

    smalls = []
    for index, (source, target) in enumerate(
        ((starts_any, starts), (bins_any, bins), (weights_any, weights))
    ):
        load = pltpu.make_async_copy(source, target, small_sem.at[index])
        load.start()
        smalls.append(load)
    loads = []
    for index, (at, size) in enumerate(STEPS):
        part = pl.ds(at * TILES, size * TILES)
        load = pltpu.make_async_copy(snap.at[part], xbuf.at[part], load_sem.at[index])
        load.start()
        loads.append(load)

    barrier = pltpu.get_barrier_semaphore()
    for step in near_steps:
        pl.semaphore_signal(barrier, inc=1, device_id=far_peer(step), device_id_type=MESH)
    for step in plane_steps:
        pl.semaphore_signal(
            barrier, inc=1, device_id=plane_peer(*step)[1], device_id_type=MESH
        )
    for load in smalls:
        load.wait()

    wide = (16, DEPTH)
    sub16 = lax.broadcasted_iota(jnp.int32, wide, 0)
    place = lax.broadcasted_iota(jnp.int32, wide, 1)
    bin_of = jnp.zeros(wide, jnp.int32)
    for freq in range(NFREQ):
        bin_of = jnp.where(sub16 == (freq % 2) * 8 + freq // 2, bins[freq], bin_of)
    wave, _ = turn_parts(place)
    scaled = (0.5 - 0.5 * wave) / math.sqrt(0.375 * BLOCK)
    cosine, sine = turn_parts(jnp.bitwise_and(bin_of * place, BLOCK - 1))
    base = jnp.concatenate([scaled * cosine, -(scaled * sine)], axis=0)
    moment = lax.broadcasted_iota(jnp.int32, (32, DEPTH), 1)
    turned = [pltpu.roll(base, jnp.bitwise_and(starts[b], DEPTH - 1), 1) for b in range(NBLK)]
    for index, (at, size) in enumerate(STEPS):
        for order, block in enumerate(active(at, size)):
            offset = moment + (at - starts[block])
            value = jnp.where((offset >= 0) & (offset < BLOCK), turned[block], 0.0)
            high, low = split(value[:, :size])
            if size < DEPTH:
                high = jnp.concatenate([high, high], axis=1)
                low = jnp.concatenate([low, jnp.zeros_like(low)], axis=1)
            tables[index][0, pl.ds(32 * order, 32), :] = high
            tables[index][1, pl.ds(32 * order, 32), :] = low

    def add_up(at, size):
        value = xbuf[pl.ds(at * TILES, size * TILES), :]
        value = jnp.sum(value.reshape(size * TILES // 32, 32, LANES), axis=0)
        value = (value[0:8] + value[8:16]) + (value[16:24] + value[24:32])
        return value[0:4] + value[4:8]

    def convert(index, middle):
        at, size = STEPS[index]
        for first in range(0, size, 16):
            for tile in range(TILES):
                lanes = slice(tile * LANES, (tile + 1) * LANES)
                value = xbuf[pl.ds((at + first) * TILES + tile, 16, stride=TILES), :]
                high, low = split(value - middle[tile : tile + 1, :])
                x_high[index][pl.ds(first, 16), lanes] = high
                if size < DEPTH:
                    x_high[index][pl.ds(size + first, 16), lanes] = low
                else:
                    x_low[index][pl.ds(first, 16), lanes] = low

    def work(*flat):
        sums_of = (flat[:NBLK], flat[NBLK:])

        def transform(index):
            blocks = active(*STEPS[index])
            passes = [(x_high[index], (0, 1))]
            if STEPS[index][1] == DEPTH:
                passes.append((x_low[index], (0,)))
            for turn, (source, kinds) in enumerate(passes):
                for side in range(2):
                    pltpu.matmul_push_rhs(
                        source[:, side * 256 : side * 256 + 256], staging_register=turn, mxu_index=side
                    )
                for order, block in enumerate(blocks):
                    for kind in kinds:
                        rows = tables[index][kind, pl.ds(32 * order, 32), :]
                        fresh = turn if order == 0 and kind == 0 else None
                        for side in range(2):
                            pltpu.matmul_acc_lhs(sums_of[side][block], rows, load_staged_rhs=fresh)

        loads[0].wait()
        sums = add_up(*STEPS[0])
        middle = sums * (1.0 / STEPS[0][1])
        convert(0, middle)
        for index in range(1, len(STEPS)):
            loads[index].wait()
            sums = sums + add_up(*STEPS[index])
            convert(index, middle)
            transform(index - 1)
        transform(len(STEPS) - 1)
        for block in range(NBLK):
            for side in range(2):
                part = pltpu.matmul_pop(sums_of[side][block])
                for p in range(2):
                    for f in range(2):
                        for tile in range(2):
                            coef_sum[
                                pl.ds((f * TILES + side * 2 + tile) * 128 + block * 16 + p * 8, 8), :
                            ] = part[
                                p * 16 + f * 8 : p * 16 + f * 8 + 8,
                                tile * LANES : (tile + 1) * LANES,
                            ]
        tile_shape = (NBLK, LANES)
        sub = lax.broadcasted_iota(jnp.int32, tile_shape, 0)
        lane = lax.broadcasted_iota(jnp.int32, tile_shape, 1)
        lean = (sums * (1.0 / TIMES) - middle) * (BLOCK / 4 / math.sqrt(0.375 * BLOCK))
        root = jnp.sqrt(weights[...])
        root_pair = jnp.concatenate([root, root], axis=0)
        lean_pair = jnp.concatenate([lean, jnp.zeros_like(lean)], axis=0)
        for tile in range(TILES):
            lanes = slice(tile * LANES, (tile + 1) * LANES)
            for p in range(2):
                for pair in range(NFREQ // 2):
                    values = []
                    for f in range(2):
                        at = (f * TILES + tile) * 128 + p * 8 + pair
                        value = coef_sum[pl.ds(at, NBLK, stride=16), :]
                        if p == 0 and pair == 0 and f == 0:
                            value = value + lean[tile : tile + 1, :]
                        values.append(value * root[tile : tile + 1, :])
                    high, low = split(jnp.concatenate(values, axis=0))
                    to = pl.ds(p * HALF + pair * 16, 16)
                    coef_high[to, lanes] = high
                    coef_low[to, lanes] = low
        for pair in range(NFREQ // 2):
            for p in range(2):
                for block in range(NBLK):
                    value = coef_sum[pl.ds(block * 16 + p * 8 + pair, 8, stride=128), :]
                    if p == 0 and pair == 0:
                        value = value + lean_pair
                    outbox[pl.ds(pair * 128 + p * 64 + block * 8, 8), :] = value * root_pair

        for side in range(2):
            lanes = slice(side * 256, side * 256 + 256)
            pltpu.matmul_push_rhs(
                coef_high[:, lanes], staging_register=0, mxu_index=side, transpose=True
            )
            pltpu.matmul_push_rhs(
                coef_low[:, lanes], staging_register=1, mxu_index=side, transpose=True
            )
        for source, rhs in ((coef_high, 0), (coef_low, None), (coef_high, 1)):
            for part in range(NBLK):
                for side in range(2):
                    pltpu.matmul_acc_lhs(
                        sums_of[side][part],
                        source[pl.ds(32 * part, 32), side * 256 : side * 256 + 256],
                        load_staged_rhs=rhs if part == 0 else None,
                    )
        gram = [
            pltpu.matmul_pop(sums_of[0][part]) + pltpu.matmul_pop(sums_of[1][part])
            for part in range(NBLK)
        ]
        real = jnp.zeros(tile_shape, jnp.float32)
        imag = jnp.zeros(tile_shape, jnp.float32)
        for freq in range(NFREQ):
            at = freq % 4 * NBLK
            up = gram[freq // 4][at : at + NBLK]
            down = gram[4 + freq // 4][at : at + NBLK]
            own = jnp.right_shift(lane, 3) == freq
            real = jnp.where(own, up[:, :HALF] + down[:, HALF:], real)
            imag = jnp.where(own, up[:, HALF:] - down[:, :HALF], imag)
        return real, imag

    real, imag = pl.run_scoped(
        work, *[pltpu.ACC(side)((32, 256), jnp.float32) for side in range(2) for _ in range(NBLK)]
    )

    tile_shape = (NBLK, LANES)
    sub = lax.broadcasted_iota(jnp.int32, tile_shape, 0)
    lane = lax.broadcasted_iota(jnp.int32, tile_shape, 1)
    count = SLABS * CELLS * along_x * along_z
    packed = jnp.where(sub <= jnp.bitwise_and(lane, 7), real, imag) * (1.0 / count)
    diagonal = jnp.right_shift(lane, 4) == sub
    rows = jnp.where(diagonal, packed, 0.0)
    for step in range(1, 8):
        turned = jnp.where(diagonal, pltpu.roll(packed, 16 * step, 1), 0.0)
        rows = rows + pltpu.roll(turned, 8 - step, 0)
    row_out[...] = rows.reshape(NBLK, 1, LANES)
    row_in[me] = row_out[band]

    pl.semaphore_wait(barrier, len(plane_steps) + len(near_steps))

    row_copies = []
    for step in plane_steps:
        peer_band, peer = plane_peer(*step)
        copy = pltpu.make_async_remote_copy(
            src_ref=row_out.at[peer_band],
            dst_ref=row_in.at[me],
            send_sem=row_send,
            recv_sem=row_recv,
            device_id=peer,
            device_id_type=MESH,
        )
        copy.start()
        row_copies.append(copy)
    mine = pltpu.make_async_copy(
        outbox.at[pl.ds(pl.multiple_of(band * 128, 128), 128)], grouped.at[band], mine_sem
    )
    mine.start()
    box_copies = []
    for step in (4, 3, 5, 2, 6, 1, 7):
        peer_band = lax.rem(band + step, bands)
        copy = pltpu.make_async_remote_copy(
            src_ref=outbox.at[pl.ds(pl.multiple_of(peer_band * 128, 128), 128)],
            dst_ref=grouped.at[band],
            send_sem=box_send,
            recv_sem=box_recv,
            device_id=(peer_band, space),
            device_id_type=MESH,
        )
        copy.start()
        box_copies.append(copy)

    for step in (relay, along_z - relay):
        pl.semaphore_signal(
            met_sem, inc=1, device_id=far_peer(step), device_id_type=MESH
        )
    arrived = row_in.at[pl.ds(0, plane - 1)]
    pltpu.make_async_copy(arrived, arrived, row_recv).wait()
    near = jnp.sum(row_in[...], axis=0)
    far_out[...] = near.reshape(1, 1, LANES)
    far_in[z_at] = near

    pl.semaphore_wait(met_sem, 2)
    far_copies = []
    for step in far_steps:
        copy = pltpu.make_async_remote_copy(
            src_ref=far_out.at[0],
            dst_ref=far_in.at[z_at],
            send_sem=far_send,
            recv_sem=far_recv,
            device_id=far_peer(step),
            device_id_type=MESH,
        )
        copy.start()
        far_copies.append(copy)
    pltpu.make_async_copy(arrived, arrived, row_send).wait()
    arrived = far_in.at[pl.ds(0, along_z - 1)]
    pltpu.make_async_copy(arrived, arrived, far_recv).wait()
    total[...] = jnp.broadcast_to(jnp.sum(far_in[...], axis=0), (8, LANES))
    pltpu.make_async_copy(arrived, arrived, far_send).wait()
    mine.wait()
    arrived = grouped.at[pl.ds(0, bands - 1)]
    pltpu.make_async_copy(arrived, arrived, box_recv).wait()
    arrived = outbox.at[pl.ds(0, (bands - 1) * 128)]
    pltpu.make_async_copy(arrived, arrived, box_send).wait()


def modes_kernel(total, grouped, factor, modes, tiles, mixed, held, tile_sem, out_sem):
    shape = (NBLK, LANES)
    sub = lax.broadcasted_iota(jnp.int32, shape, 0)
    lane = lax.broadcasted_iota(jnp.int32, shape, 1)
    packed = total[...]
    packed = jnp.where(sub < 4, packed, pltpu.roll(packed, LANES - 8, 1))

    def entry(r, c):
        return jnp.broadcast_to(packed[:, 16 * r + c : 16 * r + c + 1], shape)

    order = NBLK
    gram_real = {(r, c): entry(r, c) for r in range(order) for c in range(r, order)}
    gram_imag = {(r, c): -entry(c, r) for r in range(order) for c in range(r + 1, order)}
    inv_real, inv_imag = {}, {}
    fac = [jnp.zeros(shape, jnp.float32), jnp.zeros(shape, jnp.float32)]
    copies = []
    for k in range(order):
        pivot = gram_real[k, k]
        scale = lax.rsqrt(pivot)
        scale = scale * (1.5 - 0.5 * pivot * scale * scale)
        row_real, row_imag = {}, {}
        for c in range(k + 1, order):
            row_real[c] = gram_real[k, c] * scale
            row_imag[c] = gram_imag[k, c] * scale
        fac[0] = jnp.where(lane == 8 * k + k, pivot * scale, fac[0])
        for c in range(k + 1, order):
            fac[0] = jnp.where(lane == 8 * k + c, row_real[c], fac[0])
            fac[1] = jnp.where(lane == 8 * k + c, row_imag[c], fac[1])
        for i in range(k + 1, order):
            gram_real[i, i] = gram_real[i, i] - (
                row_real[i] * row_real[i] + row_imag[i] * row_imag[i]
            )
            for c in range(i + 1, order):
                gram_real[i, c] = gram_real[i, c] - (
                    row_real[i] * row_real[c] + row_imag[i] * row_imag[c]
                )
                gram_imag[i, c] = gram_imag[i, c] - (
                    row_real[i] * row_imag[c] - row_imag[i] * row_real[c]
                )
        for m in range(k):
            inv_real[k, m] = inv_real[k, m] * scale
            inv_imag[k, m] = inv_imag[k, m] * scale
        inv_real[k, k] = scale
        for i in range(k + 1, order):
            for m in range(k):
                inv_real[i, m] = inv_real[i, m] - (
                    row_real[i] * inv_real[k, m] + row_imag[i] * inv_imag[k, m]
                )
                inv_imag[i, m] = inv_imag[i, m] - (
                    row_real[i] * inv_imag[k, m] - row_imag[i] * inv_real[k, m]
                )
            inv_real[i, k] = -(row_real[i] * scale)
            inv_imag[i, k] = row_imag[i] * scale
        for slab in range(SLABS):
            real = inv_real[k, k] * grouped[slab, pl.ds(k * 8, 8), :]
            imag = inv_real[k, k] * grouped[slab, pl.ds(64 + k * 8, 8), :]
            for a in range(k):
                part_real = grouped[slab, pl.ds(a * 8, 8), :]
                part_imag = grouped[slab, pl.ds(64 + a * 8, 8), :]
                real = real + (inv_real[k, a] * part_real + inv_imag[k, a] * part_imag)
                imag = imag + (inv_real[k, a] * part_imag - inv_imag[k, a] * part_real)
            mixed[pl.ds(k * 128 + slab * 8, 8), :] = real
            mixed[pl.ds(k * 128 + 64 + slab * 8, 8), :] = imag
        for p in range(2):
            for row in range(8):
                held[k, p, pl.ds(row * 8, 8), :] = mixed[
                    pl.ds(k * 128 + p * 64 + row, 8, stride=8), :
                ]
        if k == order - 1:
            for p in range(2):
                for f in range(2):
                    line = jnp.broadcast_to(fac[p][4 * f : 4 * f + 1, :], shape)
                    tile = line
                    for r in range(1, order):
                        tile = jnp.where(sub == r, pltpu.roll(line, LANES - 8 * r, 1), tile)
                    tiles[f, p] = tile[:, :8]
            out = pltpu.make_async_copy(tiles, factor, tile_sem)
            out.start()
        for f in range(2):
            copy = pltpu.make_async_copy(
                held.at[k, :, pl.ds(f * 32, 32)],
                modes.at[f, :, k],
                out_sem,
            )
            copy.start()
    out.wait()
    pltpu.make_async_copy(modes, modes, out_sem).wait()


def shards(along_z, along_x, snapshots, quad_weights, freq_bins, block_starts):
    f32, bf16 = jnp.float32, jnp.bfloat16
    vmem = pltpu.VMEM
    dma = pltpu.SemaphoreType.DMA
    bands = SLABS
    grouped, total = pl.pallas_call(
        functools.partial(spectra_kernel, along_z, along_x),
        out_shape=(
            vmem((bands, 128, LANES), f32),
            vmem((8, LANES), f32),
        ),
        in_specs=[pl.BlockSpec(memory_space=pl.ANY)] * 4,
        out_specs=(pl.BlockSpec(memory_space=pltpu.VMEM), pl.BlockSpec(memory_space=pltpu.VMEM)),
        scratch_shapes=[
            vmem((TILES, LANES), f32),
            pltpu.SMEM((NFREQ,), jnp.int32),
            pltpu.SMEM((NBLK,), jnp.int32),
            vmem((TIMES * TILES, LANES), f32),
            [vmem((2, 32 * len(active(*step)), DEPTH), bf16) for step in STEPS],
            [vmem((DEPTH, CELLS), bf16) for step in STEPS],
            [vmem((DEPTH, CELLS), bf16) for step in STEPS if step[1] == DEPTH],
            vmem((ROWS * TILES, LANES), f32),
            vmem((ROWS, CELLS), bf16),
            vmem((ROWS, CELLS), bf16),
            vmem((bands * 128, LANES), f32),
            vmem((bands, 1, LANES), f32),
            vmem((along_x * bands, 1, LANES), f32),
            vmem((1, 1, LANES), f32),
            vmem((along_z, 1, LANES), f32),
            dma((len(STEPS),)),
            dma((3,)),
            dma,
            dma,
            dma,
            dma,
            dma,
            dma,
            dma,
            pltpu.SemaphoreType.REGULAR,
        ],
        compiler_params=pltpu.CompilerParams(collective_id=0, has_side_effects=True),
        name="spectra",
    )(
        snapshots.reshape(TIMES * TILES, LANES),
        quad_weights.reshape(TILES, LANES),
        freq_bins,
        block_starts,
    )
    factor, modes = pl.pallas_call(
        modes_kernel,
        out_shape=(
            jax.ShapeDtypeStruct((2, 2, NBLK, NBLK), f32),
            jax.ShapeDtypeStruct((2, 2, NBLK, 32, LANES), f32),
        ),
        in_specs=[
            pl.BlockSpec(memory_space=pltpu.VMEM),
            pl.BlockSpec(memory_space=pltpu.VMEM),
        ],
        out_specs=(
            pl.BlockSpec(memory_space=pl.ANY),
            pl.BlockSpec(memory_space=pl.ANY),
        ),
        scratch_shapes=[
            vmem((2, 2, NBLK, NBLK), f32),
            vmem((NBLK * 128, LANES), f32),
            vmem((NBLK, 2, 64, LANES), f32),
            dma,
            dma,
        ],
        name="modes",
    )(
        pltpu.with_memory_space_constraint(total, pltpu.VMEM),
        pltpu.with_memory_space_constraint(grouped, pltpu.VMEM),
    )
    modes = modes.reshape(2, 2, NBLK, TILES, SLABS, LANES).transpose(0, 1, 2, 4, 3, 5)
    return (factor, modes.reshape(2, 2, NBLK, SLABS, CELLS))


def solution(mesh):
    along_x = min(ALONG_X, mesh.shape["space"])
    along_z = mesh.shape["space"] // along_x
    placed = (P(None, "band", "space"), P("band", "space"), P(), P())
    return jax.shard_map(
        functools.partial(shards, along_z, along_x),
        mesh=mesh,
        in_specs=placed,
        out_specs=(P("band", None, None, None), P("band", None, None, None, "space")),
        check_vma=False,
    )
```

```python
import functools
import math

import jax
import jax.numpy as jnp
from jax import lax
from jax.experimental import pallas as pl
from jax.experimental.pallas import tpu as pltpu
from jax.sharding import PartitionSpec as P

BLOCK = 256
NBLK = 8
NFREQ = 16
SLABS = 8
TIMES = 1152
CELLS = 512
LANES = 128
TILES = CELLS // LANES
ROWS = 2 * NFREQ * NBLK
HALF = NFREQ * NBLK
ALONG_X = 4
MESH = pl.DeviceIdType.MESH
DEPTH = 256
STEPS = tuple((at, min(DEPTH, TIMES - at)) for at in range(0, TIMES, DEPTH))
LAST = TIMES - BLOCK
LEAST, MOST = 64, 192


def reach(block):
    first = max(LEAST * block, LAST - MOST * (NBLK - 1 - block))
    final = min(MOST * block, LAST - LEAST * (NBLK - 1 - block))
    return first, final + BLOCK


def active(at, size):
    return [b for b in range(NBLK) if reach(b)[0] < at + size and reach(b)[1] > at]


def turn_parts(turns):
    quadrant = jnp.bitwise_and(jnp.right_shift(turns + 32, 6), 3)
    rest = jnp.bitwise_and(turns + 32, 63) - 32
    angle = rest.astype(jnp.float32) * (math.pi / 128.0)
    square = angle * angle
    sine = angle + angle * square * (
        -1.6666654611e-1 + square * (8.3321608736e-3 - 1.9515295891e-4 * square)
    )
    cosine = (1.0 - 0.5 * square) + square * square * (
        4.166664568298827e-2
        + square * (-1.388731625493765e-3 + 2.443315711809948e-5 * square)
    )
    odd = jnp.bitwise_and(quadrant, 1) == 1
    first = jnp.where(odd, sine, cosine)
    second = jnp.where(odd, cosine, sine)
    flip_cos = (quadrant == 1) | (quadrant == 2)
    flip_sin = quadrant >= 2
    return jnp.where(flip_cos, -first, first), jnp.where(flip_sin, -second, second)


def split(value):
    high = value.astype(jnp.bfloat16)
    low = (value - high.astype(jnp.float32)).astype(jnp.bfloat16)
    return high, low


def spectra_kernel(
    along_z,
    along_x,
    snap,
    weights_any,
    bins_any,
    starts_any,
    grouped,
    total,
    weights,
    bins,
    starts,
    xbuf,
    tables,
    x_high,
    x_low,
    coef_sum,
    coef_high,
    coef_low,
    outbox,
    row_out,
    row_in,
    far_out,
    far_in,
    load_sem,
    small_sem,
    mine_sem,
    row_send,
    row_recv,
    far_send,
    far_recv,
    box_send,
    box_recv,
    met_sem,
):
    band = lax.axis_index("band")
    space = lax.axis_index("space")
    z_at = space // along_x
    x_at = space % along_x
    bands = SLABS
    plane = along_x * bands
    me = x_at * bands + band

    def plane_peer(dx, dy, dc):
        x_to = lax.rem(x_at + dx, along_x)
        band_to = lax.rem(band // 2 + dy, bands // 2) * 2 + lax.rem(band % 2 + dc, 2)
        return band_to, (band_to, z_at * along_x + x_to)

    def far_peer(step):
        return (band, lax.rem(z_at + step, along_z) * along_x + x_at)

    def hops(step, size):
        return min(step, size - step)

    plane_steps = [
        (dx, dy, dc)
        for dx in range(along_x)
        for dy in range(bands // 2)
        for dc in range(2)
        if dx + dy + dc > 0
    ]
    plane_steps.sort(key=lambda s: -hops(s[0], along_x) - hops(s[1], bands // 2))
    relay = max(1, along_z // 4)
    far_steps = sorted(range(1, along_z), key=lambda s: -hops(s, along_z))

    near_steps = [step for step in far_steps if hops(step, along_z) <= relay]

    smalls = []
    for index, (source, target) in enumerate(
        ((starts_any, starts), (bins_any, bins), (weights_any, weights))
    ):
        load = pltpu.make_async_copy(source, target, small_sem.at[index])
        load.start()
        smalls.append(load)
    loads = []
    for index, (at, size) in enumerate(STEPS):
        part = pl.ds(at * TILES, size * TILES)
        load = pltpu.make_async_copy(snap.at[part], xbuf.at[part], load_sem.at[index])
        load.start()
        loads.append(load)

    barrier = pltpu.get_barrier_semaphore()
    for step in near_steps:
        pl.semaphore_signal(barrier, inc=1, device_id=far_peer(step), device_id_type=MESH)
    for step in plane_steps:
        pl.semaphore_signal(
            barrier, inc=1, device_id=plane_peer(*step)[1], device_id_type=MESH
        )
    for load in smalls:
        load.wait()

    wide = (16, DEPTH)
    sub16 = lax.broadcasted_iota(jnp.int32, wide, 0)
    place = lax.broadcasted_iota(jnp.int32, wide, 1)
    bin_of = jnp.zeros(wide, jnp.int32)
    for freq in range(NFREQ):
        bin_of = jnp.where(sub16 == (freq % 2) * 8 + freq // 2, bins[freq], bin_of)
    wave, _ = turn_parts(place)
    scaled = (0.5 - 0.5 * wave) / math.sqrt(0.375 * BLOCK)
    cosine, sine = turn_parts(jnp.bitwise_and(bin_of * place, BLOCK - 1))
    base = jnp.concatenate([scaled * cosine, -(scaled * sine)], axis=0)
    moment = lax.broadcasted_iota(jnp.int32, (32, DEPTH), 1)
    turned = [pltpu.roll(base, jnp.bitwise_and(starts[b], DEPTH - 1), 1) for b in range(NBLK)]
    for index, (at, size) in enumerate(STEPS):
        for order, block in enumerate(active(at, size)):
            offset = moment + (at - starts[block])
            value = jnp.where((offset >= 0) & (offset < BLOCK), turned[block], 0.0)
            high, low = split(value[:, :size])
            if size < DEPTH:
                high = jnp.concatenate([high, high], axis=1)
                low = jnp.concatenate([low, jnp.zeros_like(low)], axis=1)
            tables[index][0, pl.ds(32 * order, 32), :] = high
            tables[index][1, pl.ds(32 * order, 32), :] = low

    def add_up(at, size):
        value = xbuf[pl.ds(at * TILES, size * TILES), :]
        value = jnp.sum(value.reshape(size * TILES // 32, 32, LANES), axis=0)
        value = (value[0:8] + value[8:16]) + (value[16:24] + value[24:32])
        return value[0:4] + value[4:8]

    def convert(index, middle):
        at, size = STEPS[index]
        for first in range(0, size, 16):
            for tile in range(TILES):
                lanes = slice(tile * LANES, (tile + 1) * LANES)
                value = xbuf[pl.ds((at + first) * TILES + tile, 16, stride=TILES), :]
                high, low = split(value - middle[tile : tile + 1, :])
                x_high[index][pl.ds(first, 16), lanes] = high
                if size < DEPTH:
                    x_high[index][pl.ds(size + first, 16), lanes] = low
                else:
                    x_low[index][pl.ds(first, 16), lanes] = low

    def work(*flat):
        sums_of = (flat[:NBLK], flat[NBLK:])

        def transform(index):
            blocks = active(*STEPS[index])
            passes = [(x_high[index], (0, 1))]
            if STEPS[index][1] == DEPTH:
                passes.append((x_low[index], (0,)))
            for turn, (source, kinds) in enumerate(passes):
                for side in range(2):
                    pltpu.matmul_push_rhs(
                        source[:, side * 256 : side * 256 + 256], staging_register=turn, mxu_index=side
                    )
                for order, block in enumerate(blocks):
                    for kind in kinds:
                        rows = tables[index][kind, pl.ds(32 * order, 32), :]
                        fresh = turn if order == 0 and kind == 0 else None
                        for side in range(2):
                            pltpu.matmul_acc_lhs(sums_of[side][block], rows, load_staged_rhs=fresh)

        loads[0].wait()
        sums = add_up(*STEPS[0])
        middle = sums * (1.0 / STEPS[0][1])
        convert(0, middle)
        for index in range(1, len(STEPS)):
            loads[index].wait()
            sums = sums + add_up(*STEPS[index])
            convert(index, middle)
            transform(index - 1)
        transform(len(STEPS) - 1)
        lean = (sums * (1.0 / TIMES) - middle) * (BLOCK / 4 / math.sqrt(0.375 * BLOCK))
        root = jnp.sqrt(weights[...])
        top = lax.broadcasted_iota(jnp.int32, (32, LANES), 0) == 0
        for block in range(NBLK):
            for side in range(2):
                part = pltpu.matmul_pop(sums_of[side][block])
                for half in range(2):
                    tile = side * 2 + half
                    lanes = slice(tile * LANES, (tile + 1) * LANES)
                    value = part[:, half * LANES : (half + 1) * LANES]
                    value = value + jnp.where(top, lean[tile : tile + 1, :], 0.0)
                    value = value * root[tile : tile + 1, :]
                    high, low = split(value)
                    coef_high[pl.ds(32 * block, 32), lanes] = high
                    coef_low[pl.ds(32 * block, 32), lanes] = low
                    for p in range(2):
                        for f in range(2):
                            to = pl.ds((f * TILES + tile) * 128 + block * 16 + p * 8, 8)
                            coef_sum[to, :] = value[p * 16 + f * 8 : p * 16 + f * 8 + 8]

        for side in range(2):
            lanes = slice(side * 256, side * 256 + 256)
            pltpu.matmul_push_rhs(
                coef_high[:, lanes], staging_register=0, mxu_index=side, transpose=True
            )
            pltpu.matmul_push_rhs(
                coef_low[:, lanes], staging_register=1, mxu_index=side, transpose=True
            )
        for source, rhs in ((coef_high, 0), (coef_low, None), (coef_high, 1)):
            for part in range(NBLK):
                for side in range(2):
                    pltpu.matmul_acc_lhs(
                        sums_of[side][part],
                        source[pl.ds(32 * part, 32), side * 256 : side * 256 + 256],
                        load_staged_rhs=rhs if part == 0 else None,
                    )
        gram = [
            pltpu.matmul_pop(sums_of[0][part]) + pltpu.matmul_pop(sums_of[1][part])
            for part in range(NBLK)
        ]
        tile_shape = (NBLK, LANES)
        sub = lax.broadcasted_iota(jnp.int32, tile_shape, 0)
        lane = lax.broadcasted_iota(jnp.int32, tile_shape, 1)
        second = jnp.bitwise_and(lane, 8) != 0
        own = (jnp.bitwise_and(lane, 7) == sub) & (jnp.bitwise_and(lane, 16) == 0)
        column = jnp.right_shift(lane, 5)
        packed = []
        for half in range(2):
            lanes = slice(half * LANES, (half + 1) * LANES)
            total_of = None
            for block in range(NBLK):
                part = gram[block][:, lanes]
                real_row = jnp.where(second, part[8:16], part[0:8])
                imag_row = jnp.where(second, part[24:32], part[16:24])
                real_next = pltpu.roll(real_row, LANES - 16, 1)
                imag_next = pltpu.roll(imag_row, LANES - 16, 1)
                value = jnp.where(
                    column + half * 4 >= block, real_row + imag_next, real_next - imag_row
                )
                value = jnp.where(own, value, 0.0)
                if block:
                    value = pltpu.roll(value, block, 1)
                total_of = value if total_of is None else total_of + value
            packed.append(total_of)
        both = packed[0] + pltpu.roll(packed[1], 16, 1)
        rows = both
        for row in range(1, NBLK):
            rows = jnp.where(sub == row, pltpu.roll(both, LANES - row, 1), rows)
        return rows

    rows = pl.run_scoped(
        work, *[pltpu.ACC(side)((32, 256), jnp.float32) for side in range(2) for _ in range(NBLK)]
    )
    rows = rows * (1.0 / (SLABS * CELLS * along_x * along_z))
    row_out[...] = rows.reshape(NBLK, 1, LANES)
    row_in[me] = row_out[band]

    pl.semaphore_wait(barrier, len(plane_steps) + len(near_steps))

    row_copies = []
    for step in plane_steps:
        peer_band, peer = plane_peer(*step)
        copy = pltpu.make_async_remote_copy(
            src_ref=row_out.at[peer_band],
            dst_ref=row_in.at[me],
            send_sem=row_send,
            recv_sem=row_recv,
            device_id=peer,
            device_id_type=MESH,
        )
        copy.start()
        row_copies.append(copy)
    for step in (relay, along_z - relay):
        pl.semaphore_signal(
            met_sem, inc=1, device_id=far_peer(step), device_id_type=MESH
        )
    for pair in range(NFREQ // 2):
        for p in range(2):
            for block in range(NBLK):
                outbox[pl.ds(pair * 128 + p * 64 + block * 8, 8), :] = coef_sum[
                    pl.ds(block * 16 + p * 8 + pair, 8, stride=128), :
                ]
    mine = pltpu.make_async_copy(
        outbox.at[pl.ds(pl.multiple_of(band * 128, 128), 128)], grouped.at[band], mine_sem
    )
    mine.start()
    box_copies = []
    for step in (4, 3, 5, 2, 6, 1, 7):
        peer_band = lax.rem(band + step, bands)
        copy = pltpu.make_async_remote_copy(
            src_ref=outbox.at[pl.ds(pl.multiple_of(peer_band * 128, 128), 128)],
            dst_ref=grouped.at[band],
            send_sem=box_send,
            recv_sem=box_recv,
            device_id=(peer_band, space),
            device_id_type=MESH,
        )
        copy.start()
        box_copies.append(copy)

    arrived = row_in.at[pl.ds(0, plane - 1)]
    pltpu.make_async_copy(arrived, arrived, row_recv).wait()
    near = jnp.sum(row_in[...], axis=0)
    far_out[...] = near.reshape(1, 1, LANES)
    far_in[z_at] = near

    pl.semaphore_wait(met_sem, 2)
    far_copies = []
    for step in far_steps:
        copy = pltpu.make_async_remote_copy(
            src_ref=far_out.at[0],
            dst_ref=far_in.at[z_at],
            send_sem=far_send,
            recv_sem=far_recv,
            device_id=far_peer(step),
            device_id_type=MESH,
        )
        copy.start()
        far_copies.append(copy)
    pltpu.make_async_copy(arrived, arrived, row_send).wait()
    mine.wait()
    arrived = grouped.at[pl.ds(0, bands - 1)]
    pltpu.make_async_copy(arrived, arrived, box_recv).wait()
    arrived = outbox.at[pl.ds(0, (bands - 1) * 128)]
    pltpu.make_async_copy(arrived, arrived, box_send).wait()
    arrived = far_in.at[pl.ds(0, along_z - 1)]
    pltpu.make_async_copy(arrived, arrived, far_send).wait()
    pltpu.make_async_copy(arrived, arrived, far_recv).wait()
    total[...] = jnp.broadcast_to(jnp.sum(far_in[...], axis=0), (8, LANES))


def modes_kernel(total, grouped, factor, modes, tiles, mixed, held, tile_sem, out_sem):
    shape = (NBLK, LANES)
    sub = lax.broadcasted_iota(jnp.int32, shape, 0)
    lane = lax.broadcasted_iota(jnp.int32, shape, 1)
    packed = total[...]
    packed = jnp.where(sub < 4, packed, pltpu.roll(packed, LANES - 8, 1))

    def entry(r, c):
        at = c % 4 * 32 + c // 4 * 16 + r
        return jnp.broadcast_to(packed[:, at : at + 1], shape)

    order = NBLK
    gram_real = {(r, c): entry(r, c) for r in range(order) for c in range(r, order)}
    gram_imag = {(r, c): -entry(c, r) for r in range(order) for c in range(r + 1, order)}
    inv_real, inv_imag = {}, {}
    fac = [jnp.zeros(shape, jnp.float32), jnp.zeros(shape, jnp.float32)]
    copies = []
    for k in range(order):
        pivot = gram_real[k, k]
        scale = lax.rsqrt(pivot)
        scale = scale * (1.5 - 0.5 * pivot * scale * scale)
        row_real, row_imag = {}, {}
        for c in range(k + 1, order):
            row_real[c] = gram_real[k, c] * scale
            row_imag[c] = gram_imag[k, c] * scale
        fac[0] = jnp.where(lane == 8 * k + k, pivot * scale, fac[0])
        for c in range(k + 1, order):
            fac[0] = jnp.where(lane == 8 * k + c, row_real[c], fac[0])
            fac[1] = jnp.where(lane == 8 * k + c, row_imag[c], fac[1])
        for i in range(k + 1, order):
            gram_real[i, i] = gram_real[i, i] - (
                row_real[i] * row_real[i] + row_imag[i] * row_imag[i]
            )
            for c in range(i + 1, order):
                gram_real[i, c] = gram_real[i, c] - (
                    row_real[i] * row_real[c] + row_imag[i] * row_imag[c]
                )
                gram_imag[i, c] = gram_imag[i, c] - (
                    row_real[i] * row_imag[c] - row_imag[i] * row_real[c]
                )
        for m in range(k):
            inv_real[k, m] = inv_real[k, m] * scale
            inv_imag[k, m] = inv_imag[k, m] * scale
        inv_real[k, k] = scale
        for i in range(k + 1, order):
            for m in range(k):
                inv_real[i, m] = inv_real[i, m] - (
                    row_real[i] * inv_real[k, m] + row_imag[i] * inv_imag[k, m]
                )
                inv_imag[i, m] = inv_imag[i, m] - (
                    row_real[i] * inv_imag[k, m] - row_imag[i] * inv_real[k, m]
                )
            inv_real[i, k] = -(row_real[i] * scale)
            inv_imag[i, k] = row_imag[i] * scale
        for slab in range(SLABS):
            real = inv_real[k, k] * grouped[slab, pl.ds(k * 8, 8), :]
            imag = inv_real[k, k] * grouped[slab, pl.ds(64 + k * 8, 8), :]
            for a in range(k):
                part_real = grouped[slab, pl.ds(a * 8, 8), :]
                part_imag = grouped[slab, pl.ds(64 + a * 8, 8), :]
                real = real + (inv_real[k, a] * part_real + inv_imag[k, a] * part_imag)
                imag = imag + (inv_real[k, a] * part_imag - inv_imag[k, a] * part_real)
            mixed[pl.ds(k * 128 + slab * 8, 8), :] = real
            mixed[pl.ds(k * 128 + 64 + slab * 8, 8), :] = imag
        for p in range(2):
            for row in range(8):
                held[k, p, pl.ds(row * 8, 8), :] = mixed[
                    pl.ds(k * 128 + p * 64 + row, 8, stride=8), :
                ]
        if k == order - 1:
            for p in range(2):
                for f in range(2):
                    line = jnp.broadcast_to(fac[p][4 * f : 4 * f + 1, :], shape)
                    tile = line
                    for r in range(1, order):
                        tile = jnp.where(sub == r, pltpu.roll(line, LANES - 8 * r, 1), tile)
                    tiles[f, p] = tile[:, :8]
            out = pltpu.make_async_copy(tiles, factor, tile_sem)
            out.start()
        for f in range(2):
            copy = pltpu.make_async_copy(
                held.at[k, :, pl.ds(f * 32, 32)],
                modes.at[f, :, k],
                out_sem,
            )
            copy.start()
    out.wait()
    pltpu.make_async_copy(modes, modes, out_sem).wait()


def shards(along_z, along_x, snapshots, quad_weights, freq_bins, block_starts):
    f32, bf16 = jnp.float32, jnp.bfloat16
    vmem = pltpu.VMEM
    dma = pltpu.SemaphoreType.DMA
    bands = SLABS
    grouped, total = pl.pallas_call(
        functools.partial(spectra_kernel, along_z, along_x),
        out_shape=(
            vmem((bands, 128, LANES), f32),
            vmem((8, LANES), f32),
        ),
        in_specs=[pl.BlockSpec(memory_space=pl.ANY)] * 4,
        out_specs=(pl.BlockSpec(memory_space=pltpu.VMEM), pl.BlockSpec(memory_space=pltpu.VMEM)),
        scratch_shapes=[
            vmem((TILES, LANES), f32),
            pltpu.SMEM((NFREQ,), jnp.int32),
            pltpu.SMEM((NBLK,), jnp.int32),
            vmem((TIMES * TILES, LANES), f32),
            [vmem((2, 32 * len(active(*step)), DEPTH), bf16) for step in STEPS],
            [vmem((DEPTH, CELLS), bf16) for step in STEPS],
            [vmem((DEPTH, CELLS), bf16) for step in STEPS if step[1] == DEPTH],
            vmem((ROWS * TILES, LANES), f32),
            vmem((ROWS, CELLS), bf16),
            vmem((ROWS, CELLS), bf16),
            vmem((bands * 128, LANES), f32),
            vmem((bands, 1, LANES), f32),
            vmem((along_x * bands, 1, LANES), f32),
            vmem((1, 1, LANES), f32),
            vmem((along_z, 1, LANES), f32),
            dma((len(STEPS),)),
            dma((3,)),
            dma,
            dma,
            dma,
            dma,
            dma,
            dma,
            dma,
            pltpu.SemaphoreType.REGULAR,
        ],
        compiler_params=pltpu.CompilerParams(collective_id=0, has_side_effects=True),
        name="spectra",
    )(
        snapshots.reshape(TIMES * TILES, LANES),
        quad_weights.reshape(TILES, LANES),
        freq_bins,
        block_starts,
    )
    factor, modes = pl.pallas_call(
        modes_kernel,
        out_shape=(
            jax.ShapeDtypeStruct((2, 2, NBLK, NBLK), f32),
            jax.ShapeDtypeStruct((2, 2, NBLK, 32, LANES), f32),
        ),
        in_specs=[
            pl.BlockSpec(memory_space=pltpu.VMEM),
            pl.BlockSpec(memory_space=pltpu.VMEM),
        ],
        out_specs=(
            pl.BlockSpec(memory_space=pl.ANY),
            pl.BlockSpec(memory_space=pl.ANY),
        ),
        scratch_shapes=[
            vmem((2, 2, NBLK, NBLK), f32),
            vmem((NBLK * 128, LANES), f32),
            vmem((NBLK, 2, 64, LANES), f32),
            dma,
            dma,
        ],
        name="modes",
    )(
        pltpu.with_memory_space_constraint(total, pltpu.VMEM),
        pltpu.with_memory_space_constraint(grouped, pltpu.VMEM),
    )
    modes = modes.reshape(2, 2, NBLK, TILES, SLABS, LANES).transpose(0, 1, 2, 4, 3, 5)
    return (factor, modes.reshape(2, 2, NBLK, SLABS, CELLS))


def solution(mesh):
    along_x = min(ALONG_X, mesh.shape["space"])
    along_z = mesh.shape["space"] // along_x
    placed = (P(None, "band", "space"), P("band", "space"), P(), P())
    return jax.shard_map(
        functools.partial(shards, along_z, along_x),
        mesh=mesh,
        in_specs=placed,
        out_specs=(P("band", None, None, None), P("band", None, None, None, "space")),
        check_vma=False,
    )
```

```python
import functools
import math

import jax
import jax.numpy as jnp
from jax import lax
from jax.experimental import pallas as pl
from jax.experimental.pallas import tpu as pltpu
from jax.sharding import PartitionSpec as P

BLOCK = 256
NBLK = 8
NFREQ = 16
SLABS = 8
TIMES = 1152
CELLS = 512
LANES = 128
TILES = CELLS // LANES
ROWS = 2 * NFREQ * NBLK
HALF = NFREQ * NBLK
ALONG_X = 4
MESH = pl.DeviceIdType.MESH
DEPTH = 256
STEPS = tuple((at, min(DEPTH, TIMES - at)) for at in range(0, TIMES, DEPTH))
LAST = TIMES - BLOCK
LEAST, MOST = 64, 192


def reach(block):
    first = max(LEAST * block, LAST - MOST * (NBLK - 1 - block))
    final = min(MOST * block, LAST - LEAST * (NBLK - 1 - block))
    return first, final + BLOCK


def active(at, size):
    return [b for b in range(NBLK) if reach(b)[0] < at + size and reach(b)[1] > at]


def turn_parts(turns):
    quadrant = jnp.bitwise_and(jnp.right_shift(turns + 32, 6), 3)
    rest = jnp.bitwise_and(turns + 32, 63) - 32
    angle = rest.astype(jnp.float32) * (math.pi / 128.0)
    square = angle * angle
    sine = angle + angle * square * (
        -1.6666654611e-1 + square * (8.3321608736e-3 - 1.9515295891e-4 * square)
    )
    cosine = (1.0 - 0.5 * square) + square * square * (
        4.166664568298827e-2
        + square * (-1.388731625493765e-3 + 2.443315711809948e-5 * square)
    )
    odd = jnp.bitwise_and(quadrant, 1) == 1
    first = jnp.where(odd, sine, cosine)
    second = jnp.where(odd, cosine, sine)
    flip_cos = (quadrant == 1) | (quadrant == 2)
    flip_sin = quadrant >= 2
    return jnp.where(flip_cos, -first, first), jnp.where(flip_sin, -second, second)


def split(value):
    high = value.astype(jnp.bfloat16)
    low = (value - high.astype(jnp.float32)).astype(jnp.bfloat16)
    return high, low


def spectra_kernel(
    along_z,
    along_x,
    snap,
    weights_any,
    bins_any,
    starts_any,
    grouped,
    total,
    weights,
    bins,
    starts,
    xbuf,
    tables,
    coef_sum,
    outbox,
    row_out,
    row_in,
    far_out,
    far_in,
    load_sem,
    small_sem,
    mine_sem,
    row_send,
    row_recv,
    far_send,
    far_recv,
    box_send,
    box_recv,
    met_sem,
):
    band = lax.axis_index("band")
    space = lax.axis_index("space")
    z_at = space // along_x
    x_at = space % along_x
    bands = SLABS
    plane = along_x * bands
    me = x_at * bands + band

    def plane_peer(dx, dy, dc):
        x_to = lax.rem(x_at + dx, along_x)
        band_to = lax.rem(band // 2 + dy, bands // 2) * 2 + lax.rem(band % 2 + dc, 2)
        return band_to, (band_to, z_at * along_x + x_to)

    def far_peer(step):
        return (band, lax.rem(z_at + step, along_z) * along_x + x_at)

    def hops(step, size):
        return min(step, size - step)

    plane_steps = [
        (dx, dy, dc)
        for dx in range(along_x)
        for dy in range(bands // 2)
        for dc in range(2)
        if dx + dy + dc > 0
    ]
    plane_steps.sort(key=lambda s: -hops(s[0], along_x) - hops(s[1], bands // 2))
    relay = max(1, along_z // 4)
    far_steps = sorted(range(1, along_z), key=lambda s: -hops(s, along_z))

    near_steps = [step for step in far_steps if hops(step, along_z) <= relay]

    smalls = []
    for index, (source, target) in enumerate(
        ((starts_any, starts), (bins_any, bins), (weights_any, weights))
    ):
        load = pltpu.make_async_copy(source, target, small_sem.at[index])
        load.start()
        smalls.append(load)
    loads = []
    for index, (at, size) in enumerate(STEPS):
        part = pl.ds(at * TILES, size * TILES)
        load = pltpu.make_async_copy(snap.at[part], xbuf.at[part], load_sem.at[index])
        load.start()
        loads.append(load)

    barrier = pltpu.get_barrier_semaphore()
    for step in near_steps:
        pl.semaphore_signal(barrier, inc=1, device_id=far_peer(step), device_id_type=MESH)
    for step in plane_steps:
        pl.semaphore_signal(
            barrier, inc=1, device_id=plane_peer(*step)[1], device_id_type=MESH
        )
    for load in smalls:
        load.wait()

    wide = (16, DEPTH)
    sub16 = lax.broadcasted_iota(jnp.int32, wide, 0)
    place = lax.broadcasted_iota(jnp.int32, wide, 1)
    bin_of = jnp.zeros(wide, jnp.int32)
    for freq in range(NFREQ):
        bin_of = jnp.where(sub16 == (freq % 2) * 8 + freq // 2, bins[freq], bin_of)
    wave, _ = turn_parts(place)
    scaled = (0.5 - 0.5 * wave) / math.sqrt(0.375 * BLOCK)
    cosine, sine = turn_parts(jnp.bitwise_and(bin_of * place, BLOCK - 1))
    base = jnp.concatenate([scaled * cosine, -(scaled * sine)], axis=0)
    moment = lax.broadcasted_iota(jnp.int32, (32, DEPTH), 1)
    turned = [pltpu.roll(base, jnp.bitwise_and(starts[b], DEPTH - 1), 1) for b in range(NBLK)]
    for index, (at, size) in enumerate(STEPS):
        for order, block in enumerate(active(at, size)):
            offset = moment + (at - starts[block])
            value = jnp.where((offset >= 0) & (offset < BLOCK), turned[block], 0.0)
            high, low = split(value[:, :size])
            if size < DEPTH:
                high = jnp.concatenate([high, high], axis=1)
                low = jnp.concatenate([low, jnp.zeros_like(low)], axis=1)
            tables[index][0, pl.ds(32 * order, 32), :] = high
            tables[index][1, pl.ds(32 * order, 32), :] = low

    def add_up(at, size):
        value = xbuf[pl.ds(at * TILES, size * TILES), :]
        value = jnp.sum(value.reshape(size * TILES // 32, 32, LANES), axis=0)
        value = (value[0:8] + value[8:16]) + (value[16:24] + value[24:32])
        return value[0:4] + value[4:8]

    def fetch(index, side, middle):
        at, size = STEPS[index]
        highs, lows = [], []
        for first in range(0, size, 16):
            values = []
            for tile in (2 * side, 2 * side + 1):
                value = xbuf[pl.ds((at + first) * TILES + tile, 16, stride=TILES), :]
                values.append(value - middle[tile : tile + 1, :])
            high, low = split(jnp.concatenate(values, axis=1))
            highs.append(high)
            lows.append(low)
        if size < DEPTH:
            return [jnp.concatenate(highs + lows, axis=0)]
        return [jnp.concatenate(highs, axis=0), jnp.concatenate(lows, axis=0)]

    def work(*flat):
        sums_of = (flat[:NBLK], flat[NBLK:])

        def push(source, register):
            for side in range(2):
                pltpu.matmul_push_rhs(source[side], staging_register=register, mxu_index=side)

        def stream(index, kinds, fresh):
            for order, block in enumerate(active(*STEPS[index])):
                for kind in kinds:
                    rows = tables[index][kind, pl.ds(32 * order, 32), :]
                    for side in range(2):
                        pltpu.matmul_acc_lhs(sums_of[side][block], rows, load_staged_rhs=fresh)
                    fresh = None

        coef_parts = {}

        def finish(block):
            for side in range(2):
                part = pltpu.matmul_pop(sums_of[side][block])
                pieces = []
                for half in range(2):
                    tile = side * 2 + half
                    value = part[:, half * LANES : (half + 1) * LANES]
                    value = value + jnp.where(top, lean[tile : tile + 1, :], 0.0)
                    value = value * root[tile : tile + 1, :]
                    pieces.append(value)
                    for p in range(2):
                        for f in range(2):
                            to = pl.ds((f * TILES + tile) * 128 + block * 16 + p * 8, 8)
                            coef_sum[to, :] = value[p * 16 + f * 8 : p * 16 + f * 8 + 8]
                coef_parts[side, block] = split(jnp.concatenate(pieces, axis=1))

        loads[0].wait()
        sums = add_up(*STEPS[0])
        middle = sums * (1.0 / STEPS[0][1])
        parts = [fetch(0, side, middle) for side in range(2)]
        push([part[0] for part in parts], 0)
        for index in range(1, len(STEPS)):
            push([part[1] for part in parts], 1)
            stream(index - 1, (0, 1), 0)
            loads[index].wait()
            sums = sums + add_up(*STEPS[index])
            parts = [fetch(index, side, middle) for side in range(2)]
            push([part[0] for part in parts], 0)
            stream(index - 1, (0,), 1)
        lean = (sums * (1.0 / TIMES) - middle) * (BLOCK / 4 / math.sqrt(0.375 * BLOCK))
        root = jnp.sqrt(weights[...])
        top = lax.broadcasted_iota(jnp.int32, (32, LANES), 0) == 0
        for block in range(NBLK):
            if block not in active(*STEPS[-1]):
                finish(block)
        stream(len(STEPS) - 1, (0, 1), 0)
        for block in active(*STEPS[-1]):
            finish(block)

        def column_of(side, kind):
            return jnp.concatenate([coef_parts[side, b][kind] for b in range(NBLK)], axis=0)

        for kind in range(2):
            for side in range(2):
                pltpu.matmul_push_rhs(
                    column_of(side, kind), staging_register=kind, mxu_index=side, transpose=True
                )
        for kind, rhs in ((0, 0), (1, None), (0, 1)):
            for part in range(NBLK):
                for side in range(2):
                    pltpu.matmul_acc_lhs(
                        sums_of[side][part],
                        coef_parts[side, part][kind],
                        load_staged_rhs=rhs if part == 0 else None,
                    )
        gram = [
            pltpu.matmul_pop(sums_of[0][part]) + pltpu.matmul_pop(sums_of[1][part])
            for part in range(NBLK)
        ]
        tile_shape = (NBLK, LANES)
        sub = lax.broadcasted_iota(jnp.int32, tile_shape, 0)
        lane = lax.broadcasted_iota(jnp.int32, tile_shape, 1)
        second = jnp.bitwise_and(lane, 8) != 0
        own = (jnp.bitwise_and(lane, 7) == sub) & (jnp.bitwise_and(lane, 16) == 0)
        column = jnp.right_shift(lane, 5)
        packed = []
        for half in range(2):
            lanes = slice(half * LANES, (half + 1) * LANES)
            total_of = None
            for block in range(NBLK):
                part = gram[block][:, lanes]
                real_row = jnp.where(second, part[8:16], part[0:8])
                imag_row = jnp.where(second, part[24:32], part[16:24])
                real_next = pltpu.roll(real_row, LANES - 16, 1)
                imag_next = pltpu.roll(imag_row, LANES - 16, 1)
                value = jnp.where(
                    column + half * 4 >= block, real_row + imag_next, real_next - imag_row
                )
                value = jnp.where(own, value, 0.0)
                if block:
                    value = pltpu.roll(value, block, 1)
                total_of = value if total_of is None else total_of + value
            packed.append(total_of)
        both = packed[0] + pltpu.roll(packed[1], 16, 1)
        rows = both
        for row in range(1, NBLK):
            rows = jnp.where(sub == row, pltpu.roll(both, LANES - row, 1), rows)
        return rows

    rows = pl.run_scoped(
        work, *[pltpu.ACC(side)((32, 256), jnp.float32) for side in range(2) for _ in range(NBLK)]
    )
    rows = rows * (1.0 / (SLABS * CELLS * along_x * along_z))
    row_out[...] = rows.reshape(NBLK, 1, LANES)
    row_in[me] = row_out[band]

    pl.semaphore_wait(barrier, len(plane_steps) + len(near_steps))

    row_copies = []
    for step in plane_steps:
        peer_band, peer = plane_peer(*step)
        copy = pltpu.make_async_remote_copy(
            src_ref=row_out.at[peer_band],
            dst_ref=row_in.at[me],
            send_sem=row_send,
            recv_sem=row_recv,
            device_id=peer,
            device_id_type=MESH,
        )
        copy.start()
        row_copies.append(copy)
    for step in (relay, along_z - relay):
        pl.semaphore_signal(
            met_sem, inc=1, device_id=far_peer(step), device_id_type=MESH
        )
    for pair in range(NFREQ // 2):
        for p in range(2):
            for block in range(NBLK):
                outbox[pl.ds(pair * 128 + p * 64 + block * 8, 8), :] = coef_sum[
                    pl.ds(block * 16 + p * 8 + pair, 8, stride=128), :
                ]
    mine = pltpu.make_async_copy(
        outbox.at[pl.ds(pl.multiple_of(band * 128, 128), 128)], grouped.at[band], mine_sem
    )
    mine.start()
    box_copies = []
    for step in (4, 3, 5, 2, 6, 1, 7):
        peer_band = lax.rem(band + step, bands)
        copy = pltpu.make_async_remote_copy(
            src_ref=outbox.at[pl.ds(pl.multiple_of(peer_band * 128, 128), 128)],
            dst_ref=grouped.at[band],
            send_sem=box_send,
            recv_sem=box_recv,
            device_id=(peer_band, space),
            device_id_type=MESH,
        )
        copy.start()
        box_copies.append(copy)

    arrived = row_in.at[pl.ds(0, plane - 1)]
    pltpu.make_async_copy(arrived, arrived, row_recv).wait()
    near = jnp.sum(row_in[...], axis=0)
    far_out[...] = near.reshape(1, 1, LANES)
    far_in[z_at] = near

    pl.semaphore_wait(met_sem, 2)
    far_copies = []
    for step in far_steps:
        copy = pltpu.make_async_remote_copy(
            src_ref=far_out.at[0],
            dst_ref=far_in.at[z_at],
            send_sem=far_send,
            recv_sem=far_recv,
            device_id=far_peer(step),
            device_id_type=MESH,
        )
        copy.start()
        far_copies.append(copy)
    pltpu.make_async_copy(arrived, arrived, row_send).wait()
    mine.wait()
    arrived = grouped.at[pl.ds(0, bands - 1)]
    pltpu.make_async_copy(arrived, arrived, box_recv).wait()
    arrived = outbox.at[pl.ds(0, (bands - 1) * 128)]
    pltpu.make_async_copy(arrived, arrived, box_send).wait()
    arrived = far_in.at[pl.ds(0, along_z - 1)]
    pltpu.make_async_copy(arrived, arrived, far_send).wait()
    pltpu.make_async_copy(arrived, arrived, far_recv).wait()
    total[...] = jnp.broadcast_to(jnp.sum(far_in[...], axis=0), (8, LANES))


def modes_kernel(total, grouped, factor, modes, tiles, mixed, held, tile_sem, out_sem):
    shape = (NBLK, LANES)
    sub = lax.broadcasted_iota(jnp.int32, shape, 0)
    lane = lax.broadcasted_iota(jnp.int32, shape, 1)
    packed = total[...]
    packed = jnp.where(sub < 4, packed, pltpu.roll(packed, LANES - 8, 1))

    def entry(r, c):
        at = c % 4 * 32 + c // 4 * 16 + r
        return jnp.broadcast_to(packed[:, at : at + 1], shape)

    order = NBLK
    gram_real = {(r, c): entry(r, c) for r in range(order) for c in range(r, order)}
    gram_imag = {(r, c): -entry(c, r) for r in range(order) for c in range(r + 1, order)}
    inv_real, inv_imag = {}, {}
    fac = [jnp.zeros(shape, jnp.float32), jnp.zeros(shape, jnp.float32)]
    copies = []
    for k in range(order):
        pivot = gram_real[k, k]
        scale = lax.rsqrt(pivot)
        scale = scale * (1.5 - 0.5 * pivot * scale * scale)
        row_real, row_imag = {}, {}
        for c in range(k + 1, order):
            row_real[c] = gram_real[k, c] * scale
            row_imag[c] = gram_imag[k, c] * scale
        fac[0] = jnp.where(lane == 8 * k + k, pivot * scale, fac[0])
        for c in range(k + 1, order):
            fac[0] = jnp.where(lane == 8 * k + c, row_real[c], fac[0])
            fac[1] = jnp.where(lane == 8 * k + c, row_imag[c], fac[1])
        for i in range(k + 1, order):
            gram_real[i, i] = gram_real[i, i] - (
                row_real[i] * row_real[i] + row_imag[i] * row_imag[i]
            )
            for c in range(i + 1, order):
                gram_real[i, c] = gram_real[i, c] - (
                    row_real[i] * row_real[c] + row_imag[i] * row_imag[c]
                )
                gram_imag[i, c] = gram_imag[i, c] - (
                    row_real[i] * row_imag[c] - row_imag[i] * row_real[c]
                )
        for m in range(k):
            inv_real[k, m] = inv_real[k, m] * scale
            inv_imag[k, m] = inv_imag[k, m] * scale
        inv_real[k, k] = scale
        for i in range(k + 1, order):
            for m in range(k):
                inv_real[i, m] = inv_real[i, m] - (
                    row_real[i] * inv_real[k, m] + row_imag[i] * inv_imag[k, m]
                )
                inv_imag[i, m] = inv_imag[i, m] - (
                    row_real[i] * inv_imag[k, m] - row_imag[i] * inv_real[k, m]
                )
            inv_real[i, k] = -(row_real[i] * scale)
            inv_imag[i, k] = row_imag[i] * scale
        for slab in range(SLABS):
            real = inv_real[k, k] * grouped[slab, pl.ds(k * 8, 8), :]
            imag = inv_real[k, k] * grouped[slab, pl.ds(64 + k * 8, 8), :]
            for a in range(k):
                part_real = grouped[slab, pl.ds(a * 8, 8), :]
                part_imag = grouped[slab, pl.ds(64 + a * 8, 8), :]
                real = real + (inv_real[k, a] * part_real + inv_imag[k, a] * part_imag)
                imag = imag + (inv_real[k, a] * part_imag - inv_imag[k, a] * part_real)
            mixed[pl.ds(k * 128 + slab * 8, 8), :] = real
            mixed[pl.ds(k * 128 + 64 + slab * 8, 8), :] = imag
        for p in range(2):
            for row in range(8):
                held[k, p, pl.ds(row * 8, 8), :] = mixed[
                    pl.ds(k * 128 + p * 64 + row, 8, stride=8), :
                ]
        if k == order - 1:
            for p in range(2):
                for f in range(2):
                    line = jnp.broadcast_to(fac[p][4 * f : 4 * f + 1, :], shape)
                    tile = line
                    for r in range(1, order):
                        tile = jnp.where(sub == r, pltpu.roll(line, LANES - 8 * r, 1), tile)
                    tiles[f, p] = tile[:, :8]
            out = pltpu.make_async_copy(tiles, factor, tile_sem)
            out.start()
        for f in range(2):
            copy = pltpu.make_async_copy(
                held.at[k, :, pl.ds(f * 32, 32)],
                modes.at[f, :, k],
                out_sem,
            )
            copy.start()
    out.wait()
    pltpu.make_async_copy(modes, modes, out_sem).wait()


def shards(along_z, along_x, snapshots, quad_weights, freq_bins, block_starts):
    f32, bf16 = jnp.float32, jnp.bfloat16
    vmem = pltpu.VMEM
    dma = pltpu.SemaphoreType.DMA
    bands = SLABS
    grouped, total = pl.pallas_call(
        functools.partial(spectra_kernel, along_z, along_x),
        out_shape=(
            vmem((bands, 128, LANES), f32),
            vmem((8, LANES), f32),
        ),
        in_specs=[pl.BlockSpec(memory_space=pl.ANY)] * 4,
        out_specs=(pl.BlockSpec(memory_space=pltpu.VMEM), pl.BlockSpec(memory_space=pltpu.VMEM)),
        scratch_shapes=[
            vmem((TILES, LANES), f32),
            pltpu.SMEM((NFREQ,), jnp.int32),
            pltpu.SMEM((NBLK,), jnp.int32),
            vmem((TIMES * TILES, LANES), f32),
            [vmem((2, 32 * len(active(*step)), DEPTH), bf16) for step in STEPS],
            vmem((ROWS * TILES, LANES), f32),
            vmem((bands * 128, LANES), f32),
            vmem((bands, 1, LANES), f32),
            vmem((along_x * bands, 1, LANES), f32),
            vmem((1, 1, LANES), f32),
            vmem((along_z, 1, LANES), f32),
            dma((len(STEPS),)),
            dma((3,)),
            dma,
            dma,
            dma,
            dma,
            dma,
            dma,
            dma,
            pltpu.SemaphoreType.REGULAR,
        ],
        compiler_params=pltpu.CompilerParams(collective_id=0, has_side_effects=True),
        name="spectra",
    )(
        snapshots.reshape(TIMES * TILES, LANES),
        quad_weights.reshape(TILES, LANES),
        freq_bins,
        block_starts,
    )
    factor, modes = pl.pallas_call(
        modes_kernel,
        out_shape=(
            jax.ShapeDtypeStruct((2, 2, NBLK, NBLK), f32),
            jax.ShapeDtypeStruct((2, 2, NBLK, 32, LANES), f32),
        ),
        in_specs=[
            pl.BlockSpec(memory_space=pltpu.VMEM),
            pl.BlockSpec(memory_space=pltpu.VMEM),
        ],
        out_specs=(
            pl.BlockSpec(memory_space=pl.ANY),
            pl.BlockSpec(memory_space=pl.ANY),
        ),
        scratch_shapes=[
            vmem((2, 2, NBLK, NBLK), f32),
            vmem((NBLK * 128, LANES), f32),
            vmem((NBLK, 2, 64, LANES), f32),
            dma,
            dma,
        ],
        name="modes",
    )(
        pltpu.with_memory_space_constraint(total, pltpu.VMEM),
        pltpu.with_memory_space_constraint(grouped, pltpu.VMEM),
    )
    modes = modes.reshape(2, 2, NBLK, TILES, SLABS, LANES).transpose(0, 1, 2, 4, 3, 5)
    return (factor, modes.reshape(2, 2, NBLK, SLABS, CELLS))


def solution(mesh):
    along_x = min(ALONG_X, mesh.shape["space"])
    along_z = mesh.shape["space"] // along_x
    placed = (P(None, "band", "space"), P("band", "space"), P(), P())
    return jax.shard_map(
        functools.partial(shards, along_z, along_x),
        mesh=mesh,
        in_specs=placed,
        out_specs=(P("band", None, None, None), P("band", None, None, None, "space")),
        check_vma=False,
    )
```

```python
import functools
import math

import jax
import jax.numpy as jnp
from jax import lax
from jax.experimental import pallas as pl
from jax.experimental.pallas import tpu as pltpu
from jax.sharding import PartitionSpec as P

BLOCK = 256
NBLK = 8
NFREQ = 16
SLABS = 8
TIMES = 1152
CELLS = 512
LANES = 128
TILES = CELLS // LANES
ROWS = 2 * NFREQ * NBLK
HALF = NFREQ * NBLK
ALONG_X = 4
MESH = pl.DeviceIdType.MESH
DEPTH = 256
STEPS = tuple((at, min(DEPTH, TIMES - at)) for at in range(0, TIMES, DEPTH))
LAST = TIMES - BLOCK
LEAST, MOST = 64, 192


def reach(block):
    first = max(LEAST * block, LAST - MOST * (NBLK - 1 - block))
    final = min(MOST * block, LAST - LEAST * (NBLK - 1 - block))
    return first, final + BLOCK


def active(at, size):
    return [b for b in range(NBLK) if reach(b)[0] < at + size and reach(b)[1] > at]


def turn_parts(turns):
    quadrant = jnp.bitwise_and(jnp.right_shift(turns + 32, 6), 3)
    rest = jnp.bitwise_and(turns + 32, 63) - 32
    angle = rest.astype(jnp.float32) * (math.pi / 128.0)
    square = angle * angle
    sine = angle + angle * square * (
        -1.6666654611e-1 + square * (8.3321608736e-3 - 1.9515295891e-4 * square)
    )
    cosine = (1.0 - 0.5 * square) + square * square * (
        4.166664568298827e-2
        + square * (-1.388731625493765e-3 + 2.443315711809948e-5 * square)
    )
    odd = jnp.bitwise_and(quadrant, 1) == 1
    first = jnp.where(odd, sine, cosine)
    second = jnp.where(odd, cosine, sine)
    flip_cos = (quadrant == 1) | (quadrant == 2)
    flip_sin = quadrant >= 2
    return jnp.where(flip_cos, -first, first), jnp.where(flip_sin, -second, second)


def split(value):
    high = value.astype(jnp.bfloat16)
    low = (value - high.astype(jnp.float32)).astype(jnp.bfloat16)
    return high, low


def spectra_body(
    along_z,
    along_x,
    snap,
    weights_any,
    bins_any,
    starts_any,
    grouped,
    total,
    weights,
    bins,
    starts,
    xbuf,
    tables,
    coef_sum,
    outbox,
    row_out,
    row_in,
    far_out,
    far_in,
    row_recv,
    far_recv,
    box_recv,
    met_sem,
    *,
    load_sem,
    small_sem,
    mine_sem,
    row_send,
    far_send,
    box_send,
):
    band = lax.axis_index("band")
    space = lax.axis_index("space")
    z_at = space // along_x
    x_at = space % along_x
    bands = SLABS
    plane = along_x * bands
    me = x_at * bands + band

    def plane_peer(dx, dy, dc):
        x_to = lax.rem(x_at + dx, along_x)
        band_to = lax.rem(band // 2 + dy, bands // 2) * 2 + lax.rem(band % 2 + dc, 2)
        return band_to, (band_to, z_at * along_x + x_to)

    def far_peer(step):
        return (band, lax.rem(z_at + step, along_z) * along_x + x_at)

    def hops(step, size):
        return min(step, size - step)

    plane_steps = [
        (dx, dy, dc)
        for dx in range(along_x)
        for dy in range(bands // 2)
        for dc in range(2)
        if dx + dy + dc > 0
    ]
    plane_steps.sort(key=lambda s: -hops(s[0], along_x) - hops(s[1], bands // 2))
    relay = max(1, along_z // 4)
    far_steps = sorted(range(1, along_z), key=lambda s: -hops(s, along_z))

    near_steps = [step for step in far_steps if hops(step, along_z) <= relay]

    smalls = []
    for index, (source, target) in enumerate(
        ((starts_any, starts), (bins_any, bins), (weights_any, weights))
    ):
        load = pltpu.make_async_copy(source, target, small_sem.at[index])
        load.start()
        smalls.append(load)
    loads = []
    for index, (at, size) in enumerate(STEPS):
        part = pl.ds(at * TILES, size * TILES)
        load = pltpu.make_async_copy(snap.at[part], xbuf.at[part], load_sem.at[index])
        load.start()
        loads.append(load)

    barrier = pltpu.get_barrier_semaphore()
    for step in near_steps:
        pl.semaphore_signal(barrier, inc=1, device_id=far_peer(step), device_id_type=MESH)
    for step in plane_steps:
        pl.semaphore_signal(
            barrier, inc=1, device_id=plane_peer(*step)[1], device_id_type=MESH
        )
    for load in smalls:
        load.wait()

    wide = (16, DEPTH)
    sub16 = lax.broadcasted_iota(jnp.int32, wide, 0)
    place = lax.broadcasted_iota(jnp.int32, wide, 1)
    bin_of = jnp.zeros(wide, jnp.int32)
    for freq in range(NFREQ):
        bin_of = jnp.where(sub16 == (freq % 2) * 8 + freq // 2, bins[freq], bin_of)
    wave, _ = turn_parts(place)
    scaled = (0.5 - 0.5 * wave) / math.sqrt(0.375 * BLOCK)
    cosine, sine = turn_parts(jnp.bitwise_and(bin_of * place, BLOCK - 1))
    base = jnp.concatenate([scaled * cosine, -(scaled * sine)], axis=0)
    moment = lax.broadcasted_iota(jnp.int32, (32, DEPTH), 1)
    turned = [pltpu.roll(base, jnp.bitwise_and(starts[b], DEPTH - 1), 1) for b in range(NBLK)]
    for index, (at, size) in enumerate(STEPS):
        for order, block in enumerate(active(at, size)):
            offset = moment + (at - starts[block])
            value = jnp.where((offset >= 0) & (offset < BLOCK), turned[block], 0.0)
            high, low = split(value[:, :size])
            if size < DEPTH:
                high = jnp.concatenate([high, high], axis=1)
                low = jnp.concatenate([low, jnp.zeros_like(low)], axis=1)
            tables[index][0, pl.ds(32 * order, 32), :] = high
            tables[index][1, pl.ds(32 * order, 32), :] = low

    def add_up(at, size):
        value = xbuf[pl.ds(at * TILES, size * TILES), :]
        value = jnp.sum(value.reshape(size * TILES // 32, 32, LANES), axis=0)
        value = (value[0:8] + value[8:16]) + (value[16:24] + value[24:32])
        return value[0:4] + value[4:8]

    def fetch(index, side, middle):
        at, size = STEPS[index]
        highs, lows = [], []
        for first in range(0, size, 16):
            values = []
            for tile in (2 * side, 2 * side + 1):
                value = xbuf[pl.ds((at + first) * TILES + tile, 16, stride=TILES), :]
                values.append(value - middle[tile : tile + 1, :])
            high, low = split(jnp.concatenate(values, axis=1))
            highs.append(high)
            lows.append(low)
        if size < DEPTH:
            return [jnp.concatenate(highs + lows, axis=0)]
        return [jnp.concatenate(highs, axis=0), jnp.concatenate(lows, axis=0)]

    def work(*flat):
        sums_of = (flat[:NBLK], flat[NBLK:])

        def push(source, register):
            for side in range(2):
                pltpu.matmul_push_rhs(source[side], staging_register=register, mxu_index=side)

        def stream(index, kinds, fresh):
            for order, block in enumerate(active(*STEPS[index])):
                for kind in kinds:
                    rows = tables[index][kind, pl.ds(32 * order, 32), :]
                    for side in range(2):
                        pltpu.matmul_acc_lhs(sums_of[side][block], rows, load_staged_rhs=fresh)
                    fresh = None

        coef_parts = {}

        def finish(block):
            for side in range(2):
                part = pltpu.matmul_pop(sums_of[side][block])
                pieces = []
                for half in range(2):
                    tile = side * 2 + half
                    value = part[:, half * LANES : (half + 1) * LANES]
                    value = value + jnp.where(top, lean[tile : tile + 1, :], 0.0)
                    value = value * root[tile : tile + 1, :]
                    pieces.append(value)
                    for p in range(2):
                        for f in range(2):
                            to = pl.ds((f * TILES + tile) * 128 + block * 16 + p * 8, 8)
                            coef_sum[to, :] = value[p * 16 + f * 8 : p * 16 + f * 8 + 8]
                coef_parts[side, block] = split(jnp.concatenate(pieces, axis=1))

        loads[0].wait()
        sums = add_up(*STEPS[0])
        middle = sums * (1.0 / STEPS[0][1])
        parts = [fetch(0, side, middle) for side in range(2)]
        push([part[0] for part in parts], 0)
        for index in range(1, len(STEPS)):
            push([part[1] for part in parts], 1)
            stream(index - 1, (0, 1), 0)
            loads[index].wait()
            sums = sums + add_up(*STEPS[index])
            parts = [fetch(index, side, middle) for side in range(2)]
            push([part[0] for part in parts], 0)
            stream(index - 1, (0,), 1)
        lean = (sums * (1.0 / TIMES) - middle) * (BLOCK / 4 / math.sqrt(0.375 * BLOCK))
        root = jnp.sqrt(weights[...])
        top = lax.broadcasted_iota(jnp.int32, (32, LANES), 0) == 0
        for block in range(NBLK):
            if block not in active(*STEPS[-1]):
                finish(block)
        stream(len(STEPS) - 1, (0, 1), 0)
        for block in active(*STEPS[-1]):
            finish(block)

        def column_of(side, kind):
            return jnp.concatenate([coef_parts[side, b][kind] for b in range(NBLK)], axis=0)

        for kind in range(2):
            for side in range(2):
                pltpu.matmul_push_rhs(
                    column_of(side, kind), staging_register=kind, mxu_index=side, transpose=True
                )
        for kind, rhs in ((0, 0), (1, None), (0, 1)):
            for part in range(NBLK):
                for side in range(2):
                    pltpu.matmul_acc_lhs(
                        sums_of[side][part],
                        coef_parts[side, part][kind],
                        load_staged_rhs=rhs if part == 0 else None,
                    )
        gram = [
            pltpu.matmul_pop(sums_of[0][part]) + pltpu.matmul_pop(sums_of[1][part])
            for part in range(NBLK)
        ]
        tile_shape = (NBLK, LANES)
        sub = lax.broadcasted_iota(jnp.int32, tile_shape, 0)
        lane = lax.broadcasted_iota(jnp.int32, tile_shape, 1)
        second = jnp.bitwise_and(lane, 8) != 0
        own = (jnp.bitwise_and(lane, 7) == sub) & (jnp.bitwise_and(lane, 16) == 0)
        column = jnp.right_shift(lane, 5)
        packed = []
        for half in range(2):
            lanes = slice(half * LANES, (half + 1) * LANES)
            total_of = None
            for block in range(NBLK):
                part = gram[block][:, lanes]
                real_row = jnp.where(second, part[8:16], part[0:8])
                imag_row = jnp.where(second, part[24:32], part[16:24])
                real_next = pltpu.roll(real_row, LANES - 16, 1)
                imag_next = pltpu.roll(imag_row, LANES - 16, 1)
                value = jnp.where(
                    column + half * 4 >= block, real_row + imag_next, real_next - imag_row
                )
                value = jnp.where(own, value, 0.0)
                if block:
                    value = pltpu.roll(value, block, 1)
                total_of = value if total_of is None else total_of + value
            packed.append(total_of)
        both = packed[0] + pltpu.roll(packed[1], 16, 1)
        rows = both
        for row in range(1, NBLK):
            rows = jnp.where(sub == row, pltpu.roll(both, LANES - row, 1), rows)
        return rows

    rows = pl.run_scoped(
        work, *[pltpu.ACC(side)((32, 256), jnp.float32) for side in range(2) for _ in range(NBLK)]
    )
    rows = rows * (1.0 / (SLABS * CELLS * along_x * along_z))
    row_out[...] = rows.reshape(NBLK, 1, LANES)
    row_in[me] = row_out[band]

    pl.semaphore_wait(barrier, len(plane_steps) + len(near_steps))

    row_copies = []
    for step in plane_steps:
        peer_band, peer = plane_peer(*step)
        copy = pltpu.make_async_remote_copy(
            src_ref=row_out.at[peer_band],
            dst_ref=row_in.at[me],
            send_sem=row_send,
            recv_sem=row_recv,
            device_id=peer,
            device_id_type=MESH,
        )
        copy.start()
        row_copies.append(copy)
    for step in (relay, along_z - relay):
        pl.semaphore_signal(
            met_sem, inc=1, device_id=far_peer(step), device_id_type=MESH
        )
    for pair in range(NFREQ // 2):
        for p in range(2):
            for block in range(NBLK):
                outbox[pl.ds(pair * 128 + p * 64 + block * 8, 8), :] = coef_sum[
                    pl.ds(block * 16 + p * 8 + pair, 8, stride=128), :
                ]
    mine = pltpu.make_async_copy(
        outbox.at[pl.ds(pl.multiple_of(band * 128, 128), 128)], grouped.at[band], mine_sem
    )
    mine.start()
    box_copies = []
    for step in (4, 3, 5, 2, 6, 1, 7):
        peer_band = lax.rem(band + step, bands)
        copy = pltpu.make_async_remote_copy(
            src_ref=outbox.at[pl.ds(pl.multiple_of(peer_band * 128, 128), 128)],
            dst_ref=grouped.at[band],
            send_sem=box_send,
            recv_sem=box_recv,
            device_id=(peer_band, space),
            device_id_type=MESH,
        )
        copy.start()
        box_copies.append(copy)

    arrived = row_in.at[pl.ds(0, plane - 1)]
    pltpu.make_async_copy(arrived, arrived, row_recv).wait()
    near = jnp.sum(row_in[...], axis=0)
    far_out[...] = near.reshape(1, 1, LANES)
    far_in[z_at] = near

    pl.semaphore_wait(met_sem, 2)
    far_copies = []
    for step in far_steps:
        copy = pltpu.make_async_remote_copy(
            src_ref=far_out.at[0],
            dst_ref=far_in.at[z_at],
            send_sem=far_send,
            recv_sem=far_recv,
            device_id=far_peer(step),
            device_id_type=MESH,
        )
        copy.start()
        far_copies.append(copy)
    pltpu.make_async_copy(arrived, arrived, row_send).wait()
    mine.wait()
    arrived = grouped.at[pl.ds(0, bands - 1)]
    pltpu.make_async_copy(arrived, arrived, box_recv).wait()
    arrived = outbox.at[pl.ds(0, (bands - 1) * 128)]
    pltpu.make_async_copy(arrived, arrived, box_send).wait()
    arrived = far_in.at[pl.ds(0, along_z - 1)]
    pltpu.make_async_copy(arrived, arrived, far_send).wait()
    pltpu.make_async_copy(arrived, arrived, far_recv).wait()
    total[...] = jnp.broadcast_to(jnp.sum(far_in[...], axis=0), (8, LANES))


def spectra_kernel(along_z, along_x, *refs):
    dma = pltpu.SemaphoreType.DMA
    pl.run_scoped(
        functools.partial(spectra_body, along_z, along_x, *refs),
        load_sem=dma((len(STEPS),)),
        small_sem=dma((3,)),
        mine_sem=dma,
        row_send=dma,
        far_send=dma,
        box_send=dma,
    )


def modes_body(total, grouped, factor, modes, tiles, mixed, held, *, tile_sem, out_sem):
    shape = (NBLK, LANES)
    sub = lax.broadcasted_iota(jnp.int32, shape, 0)
    lane = lax.broadcasted_iota(jnp.int32, shape, 1)
    packed = total[...]
    packed = jnp.where(sub < 4, packed, pltpu.roll(packed, LANES - 8, 1))

    def entry(r, c):
        at = c % 4 * 32 + c // 4 * 16 + r
        return jnp.broadcast_to(packed[:, at : at + 1], shape)

    order = NBLK
    gram_real = {(r, c): entry(r, c) for r in range(order) for c in range(r, order)}
    gram_imag = {(r, c): -entry(c, r) for r in range(order) for c in range(r + 1, order)}
    inv_real, inv_imag = {}, {}
    fac = [jnp.zeros(shape, jnp.float32), jnp.zeros(shape, jnp.float32)]
    copies = []
    for k in range(order):
        pivot = gram_real[k, k]
        scale = lax.rsqrt(pivot)
        scale = scale * (1.5 - 0.5 * pivot * scale * scale)
        row_real, row_imag = {}, {}
        for c in range(k + 1, order):
            row_real[c] = gram_real[k, c] * scale
            row_imag[c] = gram_imag[k, c] * scale
        fac[0] = jnp.where(lane == 8 * k + k, pivot * scale, fac[0])
        for c in range(k + 1, order):
            fac[0] = jnp.where(lane == 8 * k + c, row_real[c], fac[0])
            fac[1] = jnp.where(lane == 8 * k + c, row_imag[c], fac[1])
        for i in range(k + 1, order):
            gram_real[i, i] = gram_real[i, i] - (
                row_real[i] * row_real[i] + row_imag[i] * row_imag[i]
            )
            for c in range(i + 1, order):
                gram_real[i, c] = gram_real[i, c] - (
                    row_real[i] * row_real[c] + row_imag[i] * row_imag[c]
                )
                gram_imag[i, c] = gram_imag[i, c] - (
                    row_real[i] * row_imag[c] - row_imag[i] * row_real[c]
                )
        for m in range(k):
            inv_real[k, m] = inv_real[k, m] * scale
            inv_imag[k, m] = inv_imag[k, m] * scale
        inv_real[k, k] = scale
        for i in range(k + 1, order):
            for m in range(k):
                inv_real[i, m] = inv_real[i, m] - (
                    row_real[i] * inv_real[k, m] + row_imag[i] * inv_imag[k, m]
                )
                inv_imag[i, m] = inv_imag[i, m] - (
                    row_real[i] * inv_imag[k, m] - row_imag[i] * inv_real[k, m]
                )
            inv_real[i, k] = -(row_real[i] * scale)
            inv_imag[i, k] = row_imag[i] * scale
        for slab in range(SLABS):
            real = inv_real[k, k] * grouped[slab, pl.ds(k * 8, 8), :]
            imag = inv_real[k, k] * grouped[slab, pl.ds(64 + k * 8, 8), :]
            for a in range(k):
                part_real = grouped[slab, pl.ds(a * 8, 8), :]
                part_imag = grouped[slab, pl.ds(64 + a * 8, 8), :]
                real = real + (inv_real[k, a] * part_real + inv_imag[k, a] * part_imag)
                imag = imag + (inv_real[k, a] * part_imag - inv_imag[k, a] * part_real)
            mixed[pl.ds(k * 128 + slab * 8, 8), :] = real
            mixed[pl.ds(k * 128 + 64 + slab * 8, 8), :] = imag
        for p in range(2):
            for row in range(8):
                held[k, p, pl.ds(row * 8, 8), :] = mixed[
                    pl.ds(k * 128 + p * 64 + row, 8, stride=8), :
                ]
        if k == order - 1:
            for p in range(2):
                for f in range(2):
                    line = jnp.broadcast_to(fac[p][4 * f : 4 * f + 1, :], shape)
                    tile = line
                    for r in range(1, order):
                        tile = jnp.where(sub == r, pltpu.roll(line, LANES - 8 * r, 1), tile)
                    tiles[f, p] = tile[:, :8]
            out = pltpu.make_async_copy(tiles, factor, tile_sem)
            out.start()
        for f in range(2):
            copy = pltpu.make_async_copy(
                held.at[k, :, pl.ds(f * 32, 32)],
                modes.at[f, :, k],
                out_sem,
            )
            copy.start()
    out.wait()
    pltpu.make_async_copy(modes, modes, out_sem).wait()


def modes_kernel(*refs):
    dma = pltpu.SemaphoreType.DMA
    pl.run_scoped(functools.partial(modes_body, *refs), tile_sem=dma, out_sem=dma)


def shards(along_z, along_x, snapshots, quad_weights, freq_bins, block_starts):
    f32, bf16 = jnp.float32, jnp.bfloat16
    vmem = pltpu.VMEM
    dma = pltpu.SemaphoreType.DMA
    bands = SLABS
    grouped, total = pl.pallas_call(
        functools.partial(spectra_kernel, along_z, along_x),
        out_shape=(
            vmem((bands, 128, LANES), f32),
            vmem((8, LANES), f32),
        ),
        in_specs=[pl.BlockSpec(memory_space=pl.ANY)] * 4,
        out_specs=(pl.BlockSpec(memory_space=pltpu.VMEM), pl.BlockSpec(memory_space=pltpu.VMEM)),
        scratch_shapes=[
            vmem((TILES, LANES), f32),
            pltpu.SMEM((NFREQ,), jnp.int32),
            pltpu.SMEM((NBLK,), jnp.int32),
            vmem((TIMES * TILES, LANES), f32),
            [vmem((2, 32 * len(active(*step)), DEPTH), bf16) for step in STEPS],
            vmem((ROWS * TILES, LANES), f32),
            vmem((bands * 128, LANES), f32),
            vmem((bands, 1, LANES), f32),
            vmem((along_x * bands, 1, LANES), f32),
            vmem((1, 1, LANES), f32),
            vmem((along_z, 1, LANES), f32),
            dma,
            dma,
            dma,
            pltpu.SemaphoreType.REGULAR,
        ],
        compiler_params=pltpu.CompilerParams(
            collective_id=0, has_side_effects=True
        ),
        name="spectra",
    )(
        snapshots.reshape(TIMES * TILES, LANES),
        quad_weights.reshape(TILES, LANES),
        freq_bins,
        block_starts,
    )
    factor, modes = pl.pallas_call(
        modes_kernel,
        out_shape=(
            jax.ShapeDtypeStruct((2, 2, NBLK, NBLK), f32),
            jax.ShapeDtypeStruct((2, 2, NBLK, 32, LANES), f32),
        ),
        in_specs=[
            pl.BlockSpec(memory_space=pltpu.VMEM),
            pl.BlockSpec(memory_space=pltpu.VMEM),
        ],
        out_specs=(
            pl.BlockSpec(memory_space=pl.ANY),
            pl.BlockSpec(memory_space=pl.ANY),
        ),
        scratch_shapes=[
            vmem((2, 2, NBLK, NBLK), f32),
            vmem((NBLK * 128, LANES), f32),
            vmem((NBLK, 2, 64, LANES), f32),
        ],
        name="modes",
    )(
        pltpu.with_memory_space_constraint(total, pltpu.VMEM),
        pltpu.with_memory_space_constraint(grouped, pltpu.VMEM),
    )
    modes = modes.reshape(2, 2, NBLK, TILES, SLABS, LANES).transpose(0, 1, 2, 4, 3, 5)
    return (factor, modes.reshape(2, 2, NBLK, SLABS, CELLS))


def solution(mesh):
    along_x = min(ALONG_X, mesh.shape["space"])
    along_z = mesh.shape["space"] // along_x
    placed = (P(None, "band", "space"), P("band", "space"), P(), P())
    return jax.shard_map(
        functools.partial(shards, along_z, along_x),
        mesh=mesh,
        in_specs=placed,
        out_specs=(P("band", None, None, None), P("band", None, None, None, "space")),
        check_vma=False,
    )
```
